32 devices in a mesh: gx: 4 (over x, core), gy: 8 (over z, y).
Axes of the slice: x: 2, y: 2, z: 4, core: 2. Of those that a mesh axis runs over, the one named last changes fastest.
Arguments:
- points: bfloat16 [2048, 3, 256], P(('gx', 'gy')), may hold values from 0 to 1
- charges: bfloat16 [2048, 16, 256], P(('gx', 'gy')), may hold values from -6 to 6
- near_list: int32 [2048, 8], P(('gx', 'gy')), may hold values from 0 to 2047, as said below
- near_count: int32 [2048], P(('gx', 'gy')), may hold values from 1 to 8
- far_leaf: int32 [2048, 8], P(('gx', 'gy')), may hold values from 0 to 2047, as said below
- far_cluster: int32 [256, 8], P(('gx', 'gy')), may hold values from 0 to 255, as said below
- basis: bfloat16 [2048, 64, 256], P(('gx', 'gy')), may hold values from -0.375 to 0.375
- leaf_transfer: bfloat16 [2048, 4096], P(('gx', 'gy')), may hold values from -0.5 to 0.5
- cluster_transfer: bfloat16 [256, 4096], P(('gx', 'gy')), may hold values from -0.5 to 0.5
- leaf_coupling: bfloat16 [2048, 8, 4096], P(('gx', 'gy')), may hold values from -0.25 to 0.25
- cluster_coupling: bfloat16 [256, 8, 4096], P(('gx', 'gy')), may hold values from -0.25 to 0.25
- top_transfer: bfloat16 [2, 64, 64], replicated, may hold values from -0.5 to 0.5
- top_coupling: bfloat16 [2, 64, 64], replicated, may hold values from -0.75 to 0.75
Outputs:
- potential: float32 [2048, 16, 256], P(('gx', 'gy'))
The draws below stay inside these ranges and needn't reach their ends.
Inputs may be any that keep to these rules, and one draw needn't show every extreme that they name: `near_list`: every entry of row i is within 64 of i, and entry 0 is i itself. Slots of near_list from near_count on are not used. `far_leaf`: every entry of row i is within 64 of i. `far_cluster`: every entry of row c is within 8 of c.
All inputs are finite; a program needn't handle non-finite values.
Results may differ from the reference program's by a relative error of at most 0.0095.
Values may be sent and summed in bfloat16 or wider, within the bound.
A program may use at most 64 MiB of HBM per device.

```python
import jax
import jax.numpy as jnp
from jax import lax

LEAF = 256
K = 64
R = 16
NN = 8
NF = 8
LPD = 64
C1DEV = 8
NLEAF = 2048
NC1 = 256
TOPLEV = 5
N_GX = 4
N_GY = 8


def draw_lists(key, row_total, span, slot_count, self_first):
    row_ids = jnp.arange(row_total, dtype=jnp.int32)[:, None]
    offsets = jax.random.randint(key, (row_total, slot_count), -span, span + 1, dtype=jnp.int32)
    entries = jnp.clip(row_ids + offsets, 0, row_total - 1)
    slot_ids = jnp.arange(slot_count, dtype=jnp.int32)[None, :]
    forward = jnp.where(row_ids + span < row_total, row_ids + span, row_ids - span)
    backward = jnp.where(row_ids >= span, row_ids - span, row_ids + span)
    forward_slot = 1 if self_first else 0
    entries = jnp.where(slot_ids == forward_slot, forward, entries)
    entries = jnp.where(slot_ids == slot_count - 1, backward, entries)
    if self_first:
        entries = jnp.where(slot_ids == 0, row_ids, entries)
    return entries.astype(jnp.int32)


def draw_near_list(key, part):
    return draw_lists(jax.random.fold_in(key, 11), NLEAF, LPD, NN, True)


def draw_far_leaf(key, part):
    return draw_lists(jax.random.fold_in(key, 23), NLEAF, LPD, NF, False)


def draw_far_cluster(key, part):
    return draw_lists(jax.random.fold_in(key, 37), NC1, C1DEV, NF, False)


def set_ends(values, rng, smallest, top_value):
    index_at = [jax.random.randint(jax.random.fold_in(rng, axis), (), 0, length) for axis, length in enumerate(values.shape)]
    longest = values.shape.index(max(values.shape))
    beside = index_at[:longest] + [(index_at[longest] + 1) % values.shape[longest]] + index_at[longest + 1:]
    return values.at[tuple(index_at)].set(smallest).at[tuple(beside)].set(top_value)


def levels(stream_key, shape, pieces, least, largest):
    factor_of, own = 1.0, jax.random.fold_in(stream_key, 6)
    for axis_at, parts in pieces:
        draws = jnp.exp(jax.random.uniform(jax.random.fold_in(own, axis_at), (parts,), jnp.float32, least / len(pieces), largest / len(pieces)))
        factor_of = factor_of * jnp.repeat(draws, shape[axis_at] // parts).reshape([-1 if axis == axis_at else 1 for axis in range(len(shape))])
    return factor_of


def gaussian(rng, shape, scale, most, split=(), kind=jnp.bfloat16):
    drawn = scale * jax.random.normal(rng, shape, jnp.float32)
    if split:
        drawn = drawn * levels(rng, shape, split, -0.22, 0.18)
    return jnp.clip(drawn, -most, most).astype(kind)


def setup_inputs(seed: int = 0) -> dict:
    key_list = jax.random.split(jax.random.key(seed), 14)
    return {
        "points": jnp.clip(1.0 * jax.random.uniform(key_list[0], (NLEAF, 3, LEAF), jnp.float32) ** levels(key_list[0], (NLEAF, 3, LEAF), ((0, 32),), -0.2, 0.2), 0.0, 1.0).astype(jnp.bfloat16),
        "charges": gaussian(key_list[1], (NLEAF, R, LEAF), 1.0, 6.0, ((0, 32),)),
        "near_list": draw_near_list(jax.random.fold_in(key_list[13], 71), 0),
        "near_count": set_ends(jax.random.randint(key_list[3], (NLEAF,), 1, NN + 1), jax.random.fold_in(key_list[3], 1), 1, NN).astype(jnp.int32),
        "far_leaf": draw_far_leaf(jax.random.fold_in(key_list[13], 71), 0),
        "far_cluster": draw_far_cluster(jax.random.fold_in(key_list[13], 71), 0),
        "basis": gaussian(key_list[6], (NLEAF, K, LEAF), LEAF ** -0.5, 0.375, ((0, 32),)),
        "leaf_transfer": gaussian(key_list[7], (NLEAF, K * K), (2 * K) ** -0.5, 0.5, ((0, 32),)),
        "cluster_transfer": gaussian(key_list[8], (NC1, K * K), (2 * K) ** -0.5, 0.5, ((0, 32),)),
        "leaf_coupling": gaussian(key_list[9], (NLEAF, NF, K * K), (NF * K) ** -0.5, 0.25, ((0, 32),)),
        "cluster_coupling": gaussian(key_list[10], (NC1, NF, K * K), (NF * K) ** -0.5, 0.25, ((0, 32),)),
        "top_transfer": gaussian(key_list[11], (2, K, K), (2 * K) ** -0.5, 0.5),
        "top_coupling": gaussian(key_list[12], (2, K, K), K ** -0.5, 0.75),
    }


SOFTENING = 0.0025
STRENGTH = 0.0625
ROOT_TWO = 1.4142135623730951

def kernel_tile(target, source, live):
    squared = jnp.zeros((target.shape[0], target.shape[2], source.shape[2]), jnp.float32)
    for component in range(3):
        spread = target[:, component, :, None].astype(jnp.float32) - source[:, component, None, :].astype(jnp.float32)
        squared = squared + spread * spread
    values = STRENGTH / jnp.sqrt(squared + SOFTENING)
    return jnp.where(live[:, None, None], values, 0.0).astype(jnp.bfloat16)

def level_product(stack_in, matrix):
    return jnp.einsum('nrk,kp->nrp', stack_in.astype(jnp.float32), matrix.astype(jnp.float32))

def reference(points, charges, near_list, near_count, far_leaf, far_cluster, basis, leaf_transfer, cluster_transfer, leaf_coupling, cluster_coupling, top_transfer, top_coupling):
    leaf_total, rhs_count, leaf_size = charges.shape
    rank_size = basis.shape[1]
    device_total = N_GX * N_GY
    moments = jnp.einsum('lrs,lks->lrk', charges.astype(jnp.float32), basis.astype(jnp.float32)).astype(jnp.bfloat16)
    leaf_maps = leaf_transfer.reshape(leaf_total, rank_size, rank_size).astype(jnp.float32)
    raised = jnp.einsum('lrk,lkp->lrp', moments.astype(jnp.float32), leaf_maps)
    parent_mom = raised.reshape(leaf_total // 8, 8, rhs_count, rank_size).sum(axis=1).astype(jnp.bfloat16)
    parent_maps = cluster_transfer.reshape(-1, rank_size, rank_size).astype(jnp.float32)
    device_mom = jnp.einsum('crk,ckp->crp', parent_mom.astype(jnp.float32), parent_maps)
    device_mom = device_mom.reshape(device_total, C1DEV, rhs_count, rank_size).sum(axis=1).astype(jnp.bfloat16)
    upward = []
    current = device_mom
    for height in range(TOPLEV):
        upward.append(current)
        pair_view = current.reshape(-1, 2, rhs_count, rank_size)
        current = (level_product(pair_view[:, 0], top_transfer[0]) + level_product(pair_view[:, 1], top_transfer[1])).astype(jnp.bfloat16)
    local_field = jnp.zeros((1, rhs_count, rank_size), jnp.float32)
    for height in reversed(range(TOPLEV)):
        pair_view = upward[height].reshape(-1, 2, rhs_count, rank_size)
        rounded = local_field.astype(jnp.bfloat16)
        lower_child = level_product(pair_view[:, 1], top_coupling[0]) + ROOT_TWO * level_product(rounded, top_transfer[0].T)
        upper_child = level_product(pair_view[:, 0], top_coupling[1]) + ROOT_TWO * level_product(rounded, top_transfer[1].T)
        local_field = jnp.stack([lower_child, upper_child], axis=1).reshape(-1, rhs_count, rank_size)
    device_local = local_field.astype(jnp.bfloat16)
    parent_coup = cluster_coupling.reshape(-1, NF, rank_size, rank_size).astype(jnp.float32)
    parent_local = jnp.einsum('cfrk,cfkp->crp', parent_mom[far_cluster].astype(jnp.float32), parent_coup)
    spread_local = jnp.repeat(device_local, C1DEV, axis=0).astype(jnp.float32)
    parent_local = (parent_local + jnp.einsum('crp,ckp->crk', spread_local, parent_maps)).astype(jnp.bfloat16)

    def one_block(block_index):
        start = (block_index * LPD).astype(jnp.int32)

        def row_block(source_array):
            return lax.dynamic_slice_in_dim(source_array, start, LPD, 0)
        target = row_block(points)
        near_rows = row_block(near_list)
        used = row_block(near_count)

        def add_slot(slot_index, running):
            source_index = lax.dynamic_index_in_dim(near_rows, slot_index, 1, keepdims=False)
            tile = kernel_tile(target, points[source_index], slot_index < used)
            return running + jnp.einsum('lts,lrs->lrt', tile.astype(jnp.float32), charges[source_index].astype(jnp.float32))
        near_field = lax.fori_loop(0, NN, add_slot, jnp.zeros((LPD, rhs_count, leaf_size), jnp.float32))
        far_rows = row_block(far_leaf)
        leaf_coup = row_block(leaf_coupling).reshape(LPD, NF, rank_size, rank_size).astype(jnp.float32)
        above = jnp.repeat(lax.dynamic_slice_in_dim(parent_local, start // 8, LPD // 8, 0), 8, axis=0)
        leaf_local = jnp.einsum('lfrk,lfkp->lrp', moments[far_rows].astype(jnp.float32), leaf_coup)
        leaf_local = leaf_local + jnp.einsum('lrp,lkp->lrk', above.astype(jnp.float32), row_block(leaf_maps))
        leaf_local = leaf_local.astype(jnp.bfloat16)
        return near_field + jnp.einsum('lrk,lks->lrs', leaf_local.astype(jnp.float32), row_block(basis).astype(jnp.float32))
    result = lax.map(one_block, jnp.arange(leaf_total // LPD, dtype=jnp.int32))
    return result.reshape(leaf_total, rhs_count, leaf_size)
```

```python
import functools

import jax
import jax.numpy as jnp
from jax import lax
from jax.experimental import pallas as pl
from jax.experimental.pallas import tpu as pltpu
from jax.sharding import PartitionSpec as P

SOFTENING = 0.0025
ROOT_TWO = 1.4142135623730951
MESH = pl.DeviceIdType.MESH
F32 = jnp.float32
BF16 = jnp.bfloat16
SCALE = 16.0
EARLY = 3
GROUP = 8
MOMENTS_FIRST = False
EXCHANGE_MIB = 60
NEAR_MIB = 60


def dot(a, b, left=1, right=0):
    return lax.dot_general(a, b, (((left,), (right,)), ((), ())), preferred_element_type=F32)


def spread_map(parity, rank, links, side):
    lane = lax.broadcasted_iota(jnp.int32, (2 * rank, rank // 2 * links), 1)
    row = lax.broadcasted_iota(jnp.int32, (2 * rank, rank // 2 * links), 0)
    return jnp.where(row == side * rank + lane // links * 2 + parity, 1.0, 0.0).astype(BF16)


def link_mask(rows, links, lanes, per_link):
    lane = lax.broadcasted_iota(jnp.int32, (rows, lanes), 1)
    row = lax.broadcasted_iota(jnp.int32, (rows, lanes), 0)
    return jnp.where(lane % links == row // per_link, 1.0, 0.0)


def fold(product, rhs, rank):
    return product[:rhs, :rank] + product[rhs:, rank:]


def gathered_up(spreads, mask, links, rhs):
    halves = []
    for spread in spreads:
        wide = spread * mask
        halves.append(wide.reshape(links, rhs, wide.shape[1]).sum(axis=0))
    return jnp.concatenate(halves, axis=0).astype(BF16)


def block_diagonal(value):
    zero = jnp.zeros_like(value)
    upper = jnp.concatenate([value, zero], axis=1)
    lower = jnp.concatenate([zero, value], axis=1)
    return jnp.concatenate([upper, lower], axis=0).astype(BF16)


def spread_down(value, matrix, maps, mask, links, rhs):
    product = dot(block_diagonal(value), matrix, 1, 1)
    total = None
    for parity, spread in enumerate(maps):
        half = product[parity * rhs : (parity + 1) * rhs]
        tall = (jnp.concatenate([half] * links, axis=0) * mask).astype(BF16)
        part = dot(tall, spread, 1, 1)
        total = part if total is None else total + part
    return total


def put_points(table, points, at):
    for start in range(0, points.shape[1], 16):
        for axis in range(3):
            rows = points[axis, start : start + 16, :].astype(F32) * SCALE
            table[at + start : at + start + 16, axis, :] = rows


def put_columns(columns, points, source, leaf):
    turned = points[source].T
    for axis in range(3):
        wide = jnp.broadcast_to(turned[:, axis : axis + 1], (turned.shape[0], 128))
        columns[leaf, axis] = wide.astype(BF16)


def near_tiles(columns, leaf, points, sources):
    size = points.shape[2]
    softening = jnp.asarray(SOFTENING * SCALE * SCALE, BF16)
    sides = [
        [jnp.broadcast_to(points[source, axis : axis + 1, :], (16, size)).astype(BF16) for axis in range(3)]
        for source in sources
    ]
    parts = [[] for _ in sources]
    for start in range(0, size, 16):
        target = []
        for axis in range(3):
            column = columns[leaf, axis, start : start + 16, :]
            target.append(jnp.concatenate([column] * (size // 128), axis=1))
        for side, part in zip(sides, parts):
            squared = softening
            for axis in range(3):
                apart = target[axis] - side[axis]
                squared = squared + apart * apart
            part.append(lax.rsqrt(squared))
    return [jnp.concatenate(part, axis=0) for part in parts]


def near_value(columns, leaf, points, sources, charges):
    tiles = near_tiles(columns, leaf, points, sources)
    tile = jnp.concatenate(tiles, axis=1) if len(tiles) > 1 else tiles[0]
    value = jnp.concatenate(charges, axis=1) if len(charges) > 1 else charges[0]
    return dot(tile, value, 1, 1).T


def ramp(shape, axis):
    return lax.broadcasted_iota(jnp.int32, shape, axis)


def triangle(size):
    return jnp.where(ramp((size, size), 0) < ramp((size, size), 1), 1.0, 0.0).astype(BF16)


def plan(near_list, near_count, first, leaves, early):
    slots = near_list.shape[0]
    source = near_list - first
    slot = ramp((slots, leaves), 0)
    live = slot < near_count
    inside = live & (source >= 0) & (source < leaves)
    ones = jnp.where(inside, 1.0, 0.0).astype(BF16)
    rank_of = dot(triangle(slots), ones, 0, 0).astype(jnp.int32)
    chosen = []
    for place_at in range(early):
        here = inside & (rank_of == place_at)
        picked = jnp.where(here, source - leaves, 0).sum(axis=0, keepdims=True) + leaves
        chosen.append(picked)
    later = live & jnp.logical_not(inside & (rank_of < early))
    ones = jnp.where(later, 1.0, 0.0)
    before = dot(ones.astype(BF16), triangle(leaves))
    totals = jnp.broadcast_to(ones.sum(axis=1, keepdims=True), (slots, 128))
    before = before + dot(triangle(slots), totals.astype(BF16), 0, 0)[:, :1]
    spot = jnp.where(later, before, -1.0)
    row = jnp.where(source < 0, source + leaves, jnp.where(source < leaves, source + 2 * leaves, source))
    code = (row * leaves + ramp((slots, leaves), 1)).astype(F32)
    length = slots * leaves
    spot = spot.T
    code = code.T
    at = ramp((leaves, length), 1).astype(F32)
    found = jnp.zeros((leaves, length), F32)
    for index in range(slots):
        hit = spot[:, index : index + 1] == at
        found = found + jnp.where(hit, code[:, index : index + 1], 0.0)
    count = totals[:, :1].sum(axis=0, keepdims=True)
    pairs = found.sum(axis=0, keepdims=True)
    pairs = jnp.where(at[:1] < count, pairs, 2.0 * leaves * leaves)
    spare = jnp.full((1, 128), 2.0 * leaves * leaves, F32)
    tail = jnp.broadcast_to(count, (1, 128))
    return chosen, jnp.concatenate([pairs, spare, tail], axis=1).astype(jnp.int32)


def exchange_kernel(
    grid_shape,
    far_leaf_hbm,
    far_cluster_hbm,
    near_list_hbm,
    near_count_hbm,
    top_transfer_hbm,
    top_coupling_hbm,
    points_hbm,
    charges_hbm,
    basis_hbm,
    leaf_maps_hbm,
    parent_maps_hbm,
    parent_couplings_hbm,
    leaf_couplings_hbm,
    pairs,
    side_points,
    side_charges,
    partial_hbm,
    far_leaf,
    far_cluster,
    near_list,
    near_count,
    top_transfer,
    top_coupling,
    partial,
    source_points,
    columns,
    own_points,
    wide_moments,
    wide_parents,
    own_charges,
    basis,
    leaf_maps,
    parent_maps,
    parent_couplings,
    leaf_couplings,
    moment_table,
    parent_table,
    far,
    local,
    sent,
    arrived,
    chosen,
    early_source,
    send_sem,
    recv_sem,
    tree_send,
    tree_recv,
    own_sem,
):
    across, along = grid_shape
    total = across * along
    levels = total.bit_length() - 1
    me = lax.axis_index("gx") * along + lax.axis_index("gy")
    leaves, rhs, size = partial.shape
    rank = basis.shape[1]
    parents = leaf_maps.shape[0]
    links = leaves // parents

    def place(index):
        return (index // along, index % along)

    def sibling(height):
        step = 2**height
        return me + step - 2 * step * ((me // step) % 2)

    barrier = pltpu.get_barrier_semaphore()

    @pl.when(me > 0)
    def _():
        pl.semaphore_signal(barrier, inc=1, device_id=place(me - 1), device_id_type=MESH)

    @pl.when(me < total - 1)
    def _():
        pl.semaphore_signal(barrier, inc=1, device_id=place(me + 1), device_id_type=MESH)

    for height in range(levels):
        pl.semaphore_signal(barrier, inc=1, device_id=place(sibling(height)), device_id_type=MESH)

    own = [
        pltpu.make_async_copy(source, target, own_sem.at[index])
        for index, (source, target) in enumerate(
            (
                (points_hbm, own_points),
                (charges_hbm, own_charges.at[pl.ds(0, leaves)]),
                (basis_hbm, basis),
                (leaf_maps_hbm, leaf_maps),
                (parent_maps_hbm, parent_maps),
                (parent_couplings_hbm, parent_couplings),
                (leaf_couplings_hbm, leaf_couplings),
                (near_list_hbm, near_list),
                (near_count_hbm, near_count),
                (far_leaf_hbm, far_leaf),
                (far_cluster_hbm, far_cluster),
                (top_transfer_hbm, top_transfer),
                (top_coupling_hbm, top_coupling),
            )
        )
    ]
    for copy in own:
        copy.start()

    moments_of = wide_moments.shape[1]
    arrays = (
        [side_charges.at[side] for side in range(2)],
        [side_points.at[side] for side in range(2)],
        [wide_parents.at[side] for side in range(2)],
        [wide_moments.at[side] for side in range(2)],
    )
    mine = (charges_hbm, points_hbm, wide_parents.at[2], wide_moments.at[2])

    def rightward(index):
        return pltpu.make_async_remote_copy(
            src_ref=mine[index],
            dst_ref=arrays[index][0],
            send_sem=send_sem.at[index, 0],
            recv_sem=recv_sem.at[index, 0],
            device_id=place(jnp.minimum(me + 1, total - 1)),
            device_id_type=MESH,
        )

    def leftward(index):
        return pltpu.make_async_remote_copy(
            src_ref=mine[index],
            dst_ref=arrays[index][1],
            send_sem=send_sem.at[index, 1],
            recv_sem=recv_sem.at[index, 1],
            device_id=place(jnp.maximum(me - 1, 0)),
            device_id_type=MESH,
        )

    def climb(height):
        return pltpu.make_async_remote_copy(
            src_ref=sent.at[height],
            dst_ref=arrived.at[height],
            send_sem=tree_send.at[height],
            recv_sem=tree_recv.at[height],
            device_id=place(sibling(height)),
            device_id_type=MESH,
        )

    def send(indices):
        @pl.when(me < total - 1)
        def _():
            for index in indices:
                rightward(index).start()

        @pl.when(me > 0)
        def _():
            for index in indices:
                leftward(index).start()

    def settle(indices):
        @pl.when(me < total - 1)
        def _():
            for index in indices:
                rightward(index).wait_send()
                leftward(index).wait_recv()

        @pl.when(me > 0)
        def _():
            for index in indices:
                leftward(index).wait_send()
                rightward(index).wait_recv()

    pl.semaphore_wait(barrier, levels + jnp.where(me > 0, 1, 0) + jnp.where(me < total - 1, 1, 0))
    if not MOMENTS_FIRST:
        send((1, 0))

    half = leaves // 2
    maps = [[spread_map(parity, rank, links, side) for side in range(2)] for parity in range(2)]
    plain = [spread_map(parity, rank, links, 0)[:rank] for parity in range(2)]
    lanes = rank // 2 * links
    mask = link_mask(links * rhs, links, lanes, rhs)
    lane = lax.broadcasted_iota(jnp.int32, (2 * rhs, lanes), 1) % links
    masks = [jnp.where(lane == link, 1.0, 0.0).astype(BF16) for link in range(links)]

    own[1].wait()
    own[2].wait()
    group = 4

    def one_moment(step, carry):
        for inner in range(group):
            leaf = step * group + inner
            pair = [dot(own_charges[at], basis[at], 1, 1) for at in (leaf, leaf + half)]
            value = jnp.concatenate(pair, axis=1).astype(BF16)
            wide_moments[2, pl.ds(pl.multiple_of(leaf * rhs, rhs), rhs), :] = value
        return carry

    lax.fori_loop(0, half // group, one_moment, 0)
    own[3].wait()
    raised = []
    for parent in range(parents):
        first = parent * links * rhs % moments_of
        stack = wide_moments[2, first : first + links * rhs, :]
        wide = [dot(stack, maps[parity][parent * links // half]) for parity in range(2)]
        product = dot(gathered_up(wide, mask, links, rhs), leaf_maps[parent])
        raised.append(fold(product, rhs, rank))
    for parent in range(parents // 2):
        value = jnp.concatenate([raised[parent], raised[parent + parents // 2]], axis=1).astype(BF16)
        wide_parents[2, parent * rhs : (parent + 1) * rhs, :] = value
    own[4].wait()
    stack = wide_parents[2]
    wide = [jnp.concatenate([dot(stack, side) for side in sides], axis=0) for sides in maps]
    product = dot(gathered_up(wide, mask, parents, rhs), parent_maps[...])
    sent[0] = fold(product, rhs, rank).astype(BF16)
    climb(0).start()
    send((2, 3))
    if MOMENTS_FIRST:
        send((1, 0))

    @pl.when(me == 0)
    def _():
        wide_moments[0] = jnp.zeros(wide_moments.shape[1:], BF16)
        wide_parents[0] = jnp.zeros(wide_parents.shape[1:], BF16)

    @pl.when(me == total - 1)
    def _():
        wide_moments[1] = jnp.zeros(wide_moments.shape[1:], BF16)
        wide_parents[1] = jnp.zeros(wide_parents.shape[1:], BF16)

    own[7].wait()
    own[8].wait()
    picked, listed = plan(near_list[...], near_count[...], me * leaves, leaves, EARLY)
    pairs[...] = listed
    for index, value in enumerate(picked):
        chosen[index : index + 1, :leaves] = value
    choose = pltpu.make_async_copy(chosen, early_source, own_sem.at[len(own)])
    choose.start()

    own_charges[leaves] = jnp.zeros((rhs, size), BF16)
    own[0].wait()
    put_points(source_points, own_points, 0)
    source_points[leaves] = jnp.zeros(source_points.shape[1:], F32)

    def one_column(step, carry):
        for inner in range(group):
            leaf = step * group + inner
            put_columns(columns, source_points, leaf, leaf)
        return carry

    lax.fori_loop(0, leaves // group, one_column, 0)
    choose.wait()
    batch = 4

    def own_near(step, carry):
        results = []
        for inner in range(batch):
            leaf = step * batch + inner
            found = [early_source[index, leaf] for index in range(EARLY)]
            charges = [own_charges[source] for source in found]
            results.append(near_value(columns, leaf, source_points, found, charges))
        for inner in range(batch):
            partial[step * batch + inner] = results[inner]
        return carry

    def collect(table, index, row, first):
        gathered = None
        for link in range(links):
            source = index(row, link) - first
            span = table.shape[0] // 3
            at = jnp.where(source < 0, source + span, jnp.where(source < span, source + 2 * span, source))
            at = jnp.clip(at, 0, table.shape[0] - 1)
            part = table[at] * masks[link]
            gathered = part if gathered is None else gathered + part
        return gathered

    def far_leaves():
        settle((2, 3))
        for block in range(3):
            for parity in range(2):
                for side in range(2):
                    value = dot(wide_moments[block], maps[parity][side]).astype(BF16)
                    first = block * leaves + side * half
                    rows = slice(parity * rhs, (parity + 1) * rhs)
                    moment_table[first : first + half, rows, :] = value.reshape(half, rhs, value.shape[1])
                    value = dot(wide_parents[block], maps[parity][side]).astype(BF16)
                    first = block * parents + side * parents // 2
                    value = value.reshape(parents // 2, rhs, value.shape[1])
                    parent_table[first : first + parents // 2, rows, :] = value

        own[6].wait()

        def some_leaves(step, carry):
            for inner in range(8):
                leaf = step * 8 + inner
                product = dot(collect(moment_table, lambda row, link: far_leaf[link, row], leaf, me * leaves), leaf_couplings[leaf])
                far[pl.ds(pl.multiple_of(leaf * rhs, rhs), rhs), :] = fold(product, rhs, rank)
            return carry

        lax.fori_loop(0, leaves // 8, some_leaves, 0)

    for index in range(9, 13):
        own[index].wait()
    couplings = []
    sides = []
    steps = leaves // batch
    for height in range(levels):
        lax.fori_loop(steps * height // levels, steps * (height + 1) // levels, own_near, 0)
        climb(height).wait()
        side = (me // 2**height) % 2
        sides.append(side)
        other = arrived[height]
        couplings.append(dot(other, top_coupling[side]))
        if height < levels - 1:
            lifted = dot(sent[height], top_transfer[side]) + dot(other, top_transfer[1 - side])
            sent[height + 1] = lifted.astype(BF16)
            climb(height + 1).start()
    far_leaves()
    field = couplings[levels - 1]
    for height in reversed(range(levels - 1)):
        field = couplings[height] + ROOT_TWO * dot(field.astype(BF16), top_transfer[sides[height]], 1, 1)
    device_local = field.astype(BF16).astype(F32)

    own[5].wait()
    down = spread_down(device_local, parent_maps[...], plain, mask, links, rhs)
    parent_local = []
    for parent in range(parents):
        product = dot(collect(parent_table, lambda row, link: far_cluster[row, link], parent, me * parents), parent_couplings[parent])
        value = fold(product, rhs, rank) + down[parent * rhs : (parent + 1) * rhs]
        parent_local.append(value.astype(BF16).astype(F32))
    for parent in range(parents):
        down = spread_down(parent_local[parent], leaf_maps[parent], plain, mask, links, rhs)
        rows = slice(parent * links * rhs, (parent + 1) * links * rhs)
        local[rows, :] = (far[rows, :] + down).astype(BF16)

    def finish(step, carry):
        for inner in range(8):
            leaf = step * 8 + inner
            value = local[pl.ds(pl.multiple_of(leaf * rhs, rhs), rhs), :]
            partial[leaf] = partial[leaf] + dot(value, basis[leaf])
        return carry

    lax.fori_loop(0, leaves // 8, finish, 0)
    result = pltpu.make_async_copy(partial, partial_hbm, own_sem.at[len(own)])
    result.start()
    settle((0, 1))
    result.wait()


def near_kernel(
    pairs,
    points_hbm,
    charges_hbm,
    side_points_hbm,
    side_charges_hbm,
    partial_hbm,
    potential,
    points,
    charges,
    source_points,
    columns,
    sem,
):
    leaves, rhs, size = potential.shape
    length = pairs.shape[1]
    count = pairs[0, length - 128]
    copies = [
        pltpu.make_async_copy(source, target, sem.at[index])
        for index, (source, target) in enumerate(
            (
                (points_hbm, points.at[2]),
                (side_points_hbm, points.at[pl.ds(0, 2)]),
                (partial_hbm, potential),
                (charges_hbm, charges.at[pl.ds(2 * leaves, leaves)]),
                (side_charges_hbm.at[0], charges.at[pl.ds(0, leaves)]),
                (side_charges_hbm.at[1], charges.at[pl.ds(leaves, leaves)]),
            )
        )
    ]
    for copy in copies:
        copy.start()
    copies[0].wait()
    put_points(source_points, points.at[2], 2 * leaves)
    group = 4

    def one_column(step, carry):
        for inner in range(group):
            leaf = step * group + inner
            put_columns(columns, source_points, 2 * leaves + leaf, leaf)
        return carry

    lax.fori_loop(0, leaves // group, one_column, 0)
    copies[1].wait()
    for side in range(2):
        put_points(source_points, points.at[side], side * leaves)
    for copy in copies[2:]:
        copy.wait()

    def some_pairs(step, carry):
        results = []
        for inner in range(GROUP):
            at = step * GROUP + inner
            code = pairs[0, at]
            source = code // leaves
            target = code % leaves
            value = near_value(columns, target, source_points, [source], [charges[source]])
            results.append((target, jnp.where(at < count, value, 0.0)))
        for target, value in results:
            potential[target] = potential[target] + value
        return carry

    lax.fori_loop(0, (count + GROUP - 1) // GROUP, some_pairs, 0)


def stored(matrix, links):
    length = matrix.shape[-1]
    tiles = length // 128
    value = matrix.reshape(-1, links, tiles, 128).transpose(0, 2, 1, 3)
    return value.reshape(-1, tiles * links, 128)


def on_device(
    grid_shape,
    points,
    charges,
    near_list,
    near_count,
    far_leaf,
    far_cluster,
    basis,
    leaf_transfer,
    cluster_transfer,
    leaf_coupling,
    cluster_coupling,
    top_transfer,
    top_coupling,
):
    leaves, rhs, size = charges.shape
    rank = basis.shape[1]
    parents = cluster_transfer.shape[0]
    links = far_leaf.shape[1]
    slots = near_list.shape[1]
    levels = (grid_shape[0] * grid_shape[1]).bit_length() - 1
    turned = points.transpose(1, 0, 2)
    leaf_maps = stored(leaf_transfer, links)
    parent_maps = stored(cluster_transfer, links)[0]
    leaf_couplings = stored(leaf_coupling, links)
    parent_couplings = stored(cluster_coupling, links)
    hbm = pl.BlockSpec(memory_space=pl.ANY)
    shape = jax.ShapeDtypeStruct
    spread = rank // 2 * links
    length = slots * leaves + 2 * 128
    count_row = near_count.reshape(1, leaves)
    pairs, side_points, side_charges, partial = pl.pallas_call(
        functools.partial(exchange_kernel, grid_shape),
        out_shape=(
            shape((1, length), jnp.int32),
            shape((2,) + turned.shape, BF16),
            shape((2,) + charges.shape, BF16),
            shape((leaves, rhs, size), F32),
        ),
        in_specs=[hbm] * 13,
        out_specs=(pl.BlockSpec(memory_space=pltpu.VMEM), hbm, hbm, hbm),
        scratch_shapes=[
            pltpu.SMEM((links, leaves), jnp.int32),
            pltpu.SMEM((parents, links), jnp.int32),
            pltpu.VMEM((slots, leaves), jnp.int32),
            pltpu.VMEM((1, leaves), jnp.int32),
            pltpu.VMEM(top_transfer.shape, BF16),
            pltpu.VMEM(top_coupling.shape, BF16),
            pltpu.VMEM((leaves, rhs, size), F32),
            pltpu.VMEM((leaves + 1, 8, size), F32),
            pltpu.VMEM((leaves, 3, size, 128), BF16),
            pltpu.VMEM(turned.shape, BF16),
            pltpu.VMEM((3, leaves // 2 * rhs, 2 * rank), BF16),
            pltpu.VMEM((3, parents // 2 * rhs, 2 * rank), BF16),
            pltpu.VMEM((leaves + 1, rhs, size), BF16),
            pltpu.VMEM(basis.shape, BF16),
            pltpu.VMEM(leaf_maps.shape, BF16),
            pltpu.VMEM(parent_maps.shape, BF16),
            pltpu.VMEM(parent_couplings.shape, BF16),
            pltpu.VMEM(leaf_couplings.shape, BF16),
            pltpu.VMEM((3 * leaves, 2 * rhs, spread), BF16),
            pltpu.VMEM((3 * parents, 2 * rhs, spread), BF16),
            pltpu.VMEM((leaves * rhs, rank), F32),
            pltpu.VMEM((leaves * rhs, rank), BF16),
            pltpu.VMEM((levels, rhs, rank), BF16),
            pltpu.VMEM((levels, rhs, rank), BF16),
            pltpu.VMEM((8, 128), jnp.int32),
            pltpu.SMEM((8, 128), jnp.int32),
            pltpu.SemaphoreType.DMA((4, 2)),
            pltpu.SemaphoreType.DMA((4, 2)),
            pltpu.SemaphoreType.DMA((levels,)),
            pltpu.SemaphoreType.DMA((levels,)),
            pltpu.SemaphoreType.DMA((14,)),
        ],
        compiler_params=pltpu.CompilerParams(
            collective_id=0, has_side_effects=True, vmem_limit_bytes=EXCHANGE_MIB << 20
        ),
        name="exchange",
    )(
        far_leaf.T,
        far_cluster,
        near_list.T,
        count_row,
        top_transfer,
        top_coupling,
        turned,
        charges,
        basis,
        leaf_maps,
        parent_maps,
        parent_couplings,
        leaf_couplings,
    )
    return pl.pallas_call(
        near_kernel,
        out_shape=shape((leaves, rhs, size), F32),
        in_specs=[pl.BlockSpec(memory_space=pltpu.SMEM)] + [hbm] * 5,
        out_specs=pl.BlockSpec(memory_space=pltpu.VMEM),
        scratch_shapes=[
            pltpu.VMEM((3,) + turned.shape, BF16),
            pltpu.VMEM((3 * leaves, rhs, size), BF16),
            pltpu.VMEM((3 * leaves, 8, size), F32),
            pltpu.VMEM((leaves, 3, size, 128), BF16),
            pltpu.SemaphoreType.DMA((6,)),
        ],
        compiler_params=pltpu.CompilerParams(vmem_limit_bytes=NEAR_MIB << 20),
        name="near",
    )(pairs, turned, charges, side_points, side_charges, partial)


def solution(mesh):
    grid_shape = (mesh.shape["gx"], mesh.shape["gy"])
    both = ("gx", "gy")
    in_specs = (
        P(both, None, None),
        P(both, None, None),
        P(both, None),
        P(both),
        P(both, None),
        P(both, None),
        P(both, None, None),
        P(both, None),
        P(both, None),
        P(both, None, None),
        P(both, None, None),
        P(),
        P(),
    )
    return jax.shard_map(
        functools.partial(on_device, grid_shape),
        mesh=mesh,
        in_specs=in_specs,
        out_specs=P(both, None, None),
        check_vma=False,
    )
```

```python
import functools

import jax
import jax.numpy as jnp
from jax import lax
from jax.experimental import pallas as pl
from jax.experimental.pallas import tpu as pltpu
from jax.sharding import PartitionSpec as P

SOFTENING = 0.0025
ROOT_TWO = 1.4142135623730951
MESH = pl.DeviceIdType.MESH
F32 = jnp.float32
BF16 = jnp.bfloat16
SCALE = 16.0
EARLY = 3
FIRST = 8
SPLIT = 2
QUARTERS = 4
GROUP = 8
EXCHANGE_MIB = 60
NEAR_MIB = 60


def dot(a, b, left=1, right=0):
    return lax.dot_general(a, b, (((left,), (right,)), ((), ())), preferred_element_type=F32)


def spread_map(parity, rank, links, side):
    lane = lax.broadcasted_iota(jnp.int32, (2 * rank, rank // 2 * links), 1)
    row = lax.broadcasted_iota(jnp.int32, (2 * rank, rank // 2 * links), 0)
    return jnp.where(row == side * rank + lane // links * 2 + parity, 1.0, 0.0).astype(BF16)


def link_mask(rows, links, lanes, per_link):
    lane = lax.broadcasted_iota(jnp.int32, (rows, lanes), 1)
    row = lax.broadcasted_iota(jnp.int32, (rows, lanes), 0)
    return jnp.where(lane % links == row // per_link, 1.0, 0.0)


def fold(product, rhs, rank):
    return product[:rhs, :rank] + product[rhs:, rank:]


def gathered_up(spreads, mask, links, rhs):
    halves = []
    for spread in spreads:
        wide = spread * mask
        halves.append(wide.reshape(links, rhs, wide.shape[1]).sum(axis=0))
    return jnp.concatenate(halves, axis=0).astype(BF16)


def block_diagonal(value):
    zero = jnp.zeros_like(value)
    upper = jnp.concatenate([value, zero], axis=1)
    lower = jnp.concatenate([zero, value], axis=1)
    return jnp.concatenate([upper, lower], axis=0).astype(BF16)


def spread_down(value, matrix, maps, mask, links, rhs):
    product = dot(block_diagonal(value), matrix, 1, 1)
    total = None
    for parity, spread in enumerate(maps):
        half = product[parity * rhs : (parity + 1) * rhs]
        tall = (jnp.concatenate([half] * links, axis=0) * mask).astype(BF16)
        part = dot(tall, spread, 1, 1)
        total = part if total is None else total + part
    return total


def put_points(table, points, at):
    for start in range(0, points.shape[1], 16):
        for axis in range(3):
            rows = points[axis, start : start + 16, :].astype(F32) * SCALE
            table[at + start : at + start + 16, axis, :] = rows


def put_columns(columns, points, source, leaf):
    for axis in range(3):
        row = points[source, axis : axis + 1, :]
        columns[leaf, axis] = jnp.broadcast_to(row, (128, row.shape[1])).astype(BF16).T


def near_tiles(columns, leaf, points, sources):
    size = points.shape[2]
    softening = jnp.asarray(SOFTENING * SCALE * SCALE, BF16)
    sides = [
        [jnp.broadcast_to(points[source, axis : axis + 1, :], (16, size)).astype(BF16) for axis in range(3)]
        for source in sources
    ]
    parts = [[] for _ in sources]
    for start in range(0, size, 16):
        target = []
        for axis in range(3):
            column = columns[leaf, axis, start : start + 16, :]
            target.append(jnp.concatenate([column] * (size // 128), axis=1))
        for side, part in zip(sides, parts):
            squared = softening
            for axis in range(3):
                apart = target[axis] - side[axis]
                squared = squared + apart * apart
            part.append(lax.rsqrt(squared))
    return [jnp.concatenate(part, axis=0) for part in parts]


def near_value(columns, leaf, points, sources, charges):
    tiles = near_tiles(columns, leaf, points, sources)
    tile = jnp.concatenate(tiles, axis=1) if len(tiles) > 1 else tiles[0]
    value = jnp.concatenate(charges, axis=1) if len(charges) > 1 else charges[0]
    return dot(tile, value, 1, 1).T


def ramp(shape, axis):
    return lax.broadcasted_iota(jnp.int32, shape, axis)


def triangle(size):
    return jnp.where(ramp((size, size), 0) < ramp((size, size), 1), 1.0, 0.0).astype(BF16)


def plan(near_list, near_count, first, leaves, early):
    slots = near_list.shape[0]
    source = near_list - first
    slot = ramp((slots, leaves), 0)
    live = slot < near_count
    inside = live & (source >= 0) & (source < leaves)
    ones = jnp.where(inside, 1.0, 0.0).astype(BF16)
    rank_of = dot(triangle(slots), ones, 0, 0).astype(jnp.int32)
    chosen = []
    for place_at in range(early):
        here = inside & (rank_of == place_at)
        picked = jnp.where(here, source - leaves, 0).sum(axis=0, keepdims=True) + leaves
        chosen.append(picked)
    later = live & jnp.logical_not(inside & (rank_of < early))
    ones = jnp.where(later, 1.0, 0.0)
    per_leaf = jnp.broadcast_to(ones.sum(axis=0, keepdims=True), (8, leaves)).astype(BF16)
    before = dot(per_leaf, triangle(leaves)) + dot(triangle(slots), ones.astype(BF16), 0, 0)
    quarter = jnp.where(ramp((leaves, 128), 0) < ramp((leaves, 128), 1) * (leaves // QUARTERS), 1.0, 0.0)
    tail = dot(per_leaf, quarter.astype(BF16))[:1]
    count = tail[:, QUARTERS : QUARTERS + 1]
    spot = jnp.where(later, before, -1.0)
    row = jnp.where(source < 0, source + leaves, jnp.where(source < leaves, source + 2 * leaves, source))
    code = (row * leaves + ramp((slots, leaves), 1)).astype(F32)
    length = slots * leaves
    spot = spot.T
    code = code.T
    at = ramp((leaves, length), 1).astype(F32)
    found = jnp.zeros((leaves, length), F32)
    for index in range(slots):
        hit = spot[:, index : index + 1] == at
        found = found + jnp.where(hit, code[:, index : index + 1], 0.0)
    pairs = found.sum(axis=0, keepdims=True)
    pairs = jnp.where(at[:1] < count, pairs, 2.0 * leaves * leaves)
    spare = jnp.full((1, 128), 2.0 * leaves * leaves, F32)
    return chosen, jnp.concatenate([pairs, spare, tail], axis=1).astype(jnp.int32)


def exchange_kernel(
    grid_shape,
    far_leaf_hbm,
    far_cluster_hbm,
    near_list_hbm,
    near_count_hbm,
    top_transfer_hbm,
    top_coupling_hbm,
    points_hbm,
    charges_hbm,
    basis_hbm,
    leaf_maps_hbm,
    parent_maps_hbm,
    parent_couplings_hbm,
    leaf_couplings_hbm,
    pairs,
    side_points,
    side_charges,
    partial_hbm,
    columns_hbm,
    far_leaf,
    far_cluster,
    near_list,
    near_count,
    top_transfer,
    top_coupling,
    partial,
    source_points,
    columns,
    own_points,
    wide_moments,
    wide_parents,
    own_charges,
    basis,
    leaf_maps,
    parent_maps,
    parent_couplings,
    leaf_couplings,
    moment_table,
    parent_table,
    far,
    local,
    sent,
    in_row,
    in_column,
    tree,
    chosen,
    early_source,
    send_sem,
    recv_sem,
    row_send,
    row_recv,
    column_send,
    column_recv,
    own_sem,
):
    across, along = grid_shape
    total = across * along
    me = lax.axis_index("gx") * along + lax.axis_index("gy")
    leaves, rhs, size = partial.shape
    rank = basis.shape[1]
    parents = leaf_maps.shape[0]
    links = leaves // parents

    def place(index):
        return (index // along, index % along)

    barrier = pltpu.get_barrier_semaphore()

    row, column = lax.axis_index("gx"), lax.axis_index("gy")

    def beside(step):
        return (row, (column + step) % along)

    def across_from(step):
        return ((row + step) % across, column)

    for step in range(1, along):
        pl.semaphore_signal(barrier, inc=1, device_id=beside(step), device_id_type=MESH)
    for step in range(1, across):
        pl.semaphore_signal(barrier, inc=1, device_id=across_from(step), device_id_type=MESH)
    first_of_row = (column == 0) & (row > 0)
    last_of_row = (column == along - 1) & (row < across - 1)

    @pl.when(first_of_row)
    def _():
        pl.semaphore_signal(barrier, inc=1, device_id=(row - 1, along - 1), device_id_type=MESH)

    @pl.when(last_of_row)
    def _():
        pl.semaphore_signal(barrier, inc=1, device_id=(row + 1, 0), device_id_type=MESH)
    own = [
        pltpu.make_async_copy(source, target, own_sem.at[index])
        for index, (source, target) in enumerate(
            (
                (points_hbm, own_points),
                (charges_hbm, own_charges.at[pl.ds(0, leaves)]),
                (basis_hbm, basis),
                (leaf_maps_hbm, leaf_maps),
                (parent_maps_hbm, parent_maps),
                (parent_couplings_hbm, parent_couplings),
                (leaf_couplings_hbm, leaf_couplings),
                (near_list_hbm, near_list),
                (near_count_hbm, near_count),
                (far_leaf_hbm, far_leaf),
                (far_cluster_hbm, far_cluster),
                (top_transfer_hbm, top_transfer),
                (top_coupling_hbm, top_coupling),
            )
        )
    ]
    for copy in own:
        copy.start()

    moments_of = wide_moments.shape[1]
    half = leaves // 2

    first_part = leaves // FIRST

    def part_of(ref, side, late):
        if side == 0:
            return ref.at[pl.ds(0, leaves - first_part)] if late else ref.at[pl.ds(leaves - first_part, first_part)]
        return ref.at[pl.ds(first_part, leaves - first_part)] if late else ref.at[pl.ds(0, first_part)]

    arrays = (
        [part_of(side_charges.at[side], side, False) for side in range(2)],
        [side_points.at[side] for side in range(2)],
        [wide_parents.at[side] for side in range(2)],
        [wide_moments.at[side] for side in range(2)],
        [part_of(side_charges.at[side], side, True) for side in range(2)],
    )
    mine = (
        [part_of(charges_hbm, side, False) for side in range(2)],
        [points_hbm] * 2,
        [wide_parents.at[2]] * 2,
        [wide_moments.at[2]] * 2,
        [part_of(charges_hbm, side, True) for side in range(2)],
    )

    def rightward(index):
        return pltpu.make_async_remote_copy(
            src_ref=mine[index][0],
            dst_ref=arrays[index][0],
            send_sem=send_sem.at[index, 0],
            recv_sem=recv_sem.at[index, 0],
            device_id=place(jnp.minimum(me + 1, total - 1)),
            device_id_type=MESH,
        )

    def leftward(index):
        return pltpu.make_async_remote_copy(
            src_ref=mine[index][1],
            dst_ref=arrays[index][1],
            send_sem=send_sem.at[index, 1],
            recv_sem=recv_sem.at[index, 1],
            device_id=place(jnp.maximum(me - 1, 0)),
            device_id_type=MESH,
        )

    def to_row(step):
        return pltpu.make_async_remote_copy(
            src_ref=sent.at[0],
            dst_ref=in_row.at[column],
            send_sem=row_send.at[step],
            recv_sem=row_recv.at[column],
            device_id=beside(step),
            device_id_type=MESH,
        )

    def from_row(step):
        source = (column + step) % along
        return pltpu.make_async_remote_copy(
            src_ref=sent.at[0],
            dst_ref=in_row.at[source],
            send_sem=row_send.at[step],
            recv_sem=row_recv.at[source],
            device_id=beside(step),
            device_id_type=MESH,
        )

    def to_column(step):
        return pltpu.make_async_remote_copy(
            src_ref=sent.at[1],
            dst_ref=in_column.at[row],
            send_sem=column_send.at[step],
            recv_sem=column_recv.at[row],
            device_id=across_from(step),
            device_id_type=MESH,
        )

    def from_column(step):
        source = (row + step) % across
        return pltpu.make_async_remote_copy(
            src_ref=sent.at[1],
            dst_ref=in_column.at[source],
            send_sem=column_send.at[step],
            recv_sem=column_recv.at[source],
            device_id=across_from(step),
            device_id_type=MESH,
        )

    def tree_level(value, index, nodes, couple):
        side = index % 2
        tree[:nodes] = value.reshape(nodes, rhs, rank)
        couple.append((side, dot(tree[index + 1 - 2 * side], top_coupling[side])))
        pair = value.reshape(nodes // 2, 2 * rhs, rank)
        lower = pair[:, :rhs].reshape(nodes // 2 * rhs, rank)
        upper = pair[:, rhs:].reshape(nodes // 2 * rhs, rank)
        return (dot(lower, top_transfer[0]) + dot(upper, top_transfer[1])).astype(BF16)

    def send(indices):
        @pl.when(me < total - 1)
        def _():
            for index in indices:
                rightward(index).start()

        @pl.when(me > 0)
        def _():
            for index in indices:
                leftward(index).start()

    def settle(indices):
        @pl.when(me < total - 1)
        def _():
            for index in indices:
                rightward(index).wait_send()
                leftward(index).wait_recv()

        @pl.when(me > 0)
        def _():
            for index in indices:
                leftward(index).wait_send()
                rightward(index).wait_recv()

    corners = jnp.where(first_of_row | last_of_row, 1, 0)
    pl.semaphore_wait(barrier, along + across - 2 + corners)
    send((1, 0))

    maps = [[spread_map(parity, rank, links, side) for side in range(2)] for parity in range(2)]
    plain = [spread_map(parity, rank, links, 0)[:rank] for parity in range(2)]
    lanes = rank // 2 * links
    mask = link_mask(links * rhs, links, lanes, rhs)
    lane = lax.broadcasted_iota(jnp.int32, (2 * rhs, lanes), 1) % links
    masks = [jnp.where(lane == link, 1.0, 0.0).astype(BF16) for link in range(links)]

    own[1].wait()
    own[2].wait()
    group = 4

    def one_moment(step, carry):
        for inner in range(group):
            leaf = step * group + inner
            pair = [dot(own_charges[at], basis[at], 1, 1) for at in (leaf, leaf + half)]
            value = jnp.concatenate(pair, axis=1).astype(BF16)
            wide_moments[2, pl.ds(pl.multiple_of(leaf * rhs, rhs), rhs), :] = value
        return carry

    lax.fori_loop(0, half // group, one_moment, 0)
    own[3].wait()
    raised = []
    for parent in range(parents):
        first = parent * links * rhs % moments_of
        stack = wide_moments[2, first : first + links * rhs, :]
        wide = [dot(stack, maps[parity][parent * links // half]) for parity in range(2)]
        product = dot(gathered_up(wide, mask, links, rhs), leaf_maps[parent])
        raised.append(fold(product, rhs, rank))
    for parent in range(parents // 2):
        value = jnp.concatenate([raised[parent], raised[parent + parents // 2]], axis=1).astype(BF16)
        wide_parents[2, parent * rhs : (parent + 1) * rhs, :] = value
    own[4].wait()
    stack = wide_parents[2]
    wide = [jnp.concatenate([dot(stack, side) for side in sides], axis=0) for sides in maps]
    product = dot(gathered_up(wide, mask, parents, rhs), parent_maps[...])
    moment = fold(product, rhs, rank).astype(BF16)
    sent[0] = moment
    for step in range(1, along):
        to_row(step).start()
    send((2, 3))

    @pl.when(me == 0)
    def _():
        wide_moments[0] = jnp.zeros(wide_moments.shape[1:], BF16)
        wide_parents[0] = jnp.zeros(wide_parents.shape[1:], BF16)

    @pl.when(me == total - 1)
    def _():
        wide_moments[1] = jnp.zeros(wide_moments.shape[1:], BF16)
        wide_parents[1] = jnp.zeros(wide_parents.shape[1:], BF16)

    own[7].wait()
    own[8].wait()
    picked, listed = plan(near_list[...], near_count[...], me * leaves, leaves, EARLY)
    pairs[...] = listed
    for index, value in enumerate(picked):
        chosen[index : index + 1, :leaves] = value
    choose = pltpu.make_async_copy(chosen, early_source, own_sem.at[len(own)])
    choose.start()

    own_charges[leaves] = jnp.zeros((rhs, size), BF16)
    own[0].wait()
    put_points(source_points, own_points, 0)
    source_points[leaves] = jnp.zeros(source_points.shape[1:], F32)

    def one_column(step, carry):
        for inner in range(group):
            leaf = step * group + inner
            put_columns(columns, source_points, leaf, leaf)
        return carry

    lax.fori_loop(0, leaves // group, one_column, 0)
    keep = pltpu.make_async_copy(columns, columns_hbm, own_sem.at[len(own) + 1])
    keep.start()
    choose.wait()
    batch = 4

    def own_near(step, carry):
        results = []
        for inner in range(batch):
            leaf = step * batch + inner
            found = [early_source[index, leaf] for index in range(EARLY)]
            charges = [own_charges[source] for source in found]
            results.append(near_value(columns, leaf, source_points, found, charges))
        for inner in range(batch):
            partial[step * batch + inner] = results[inner]
        return carry

    def collect(table, index, row, first):
        gathered = None
        for link in range(links):
            source = index(row, link) - first
            span = table.shape[0] // 3
            at = jnp.where(source < 0, source + span, jnp.where(source < span, source + 2 * span, source))
            at = jnp.clip(at, 0, table.shape[0] - 1)
            part = table[at] * masks[link]
            gathered = part if gathered is None else gathered + part
        return gathered

    def far_leaves():
        settle((2, 3))
        for block in range(3):
            for parity in range(2):
                for side in range(2):
                    value = dot(wide_moments[block], maps[parity][side]).astype(BF16)
                    first = block * leaves + side * half
                    rows = slice(parity * rhs, (parity + 1) * rhs)
                    moment_table[first : first + half, rows, :] = value.reshape(half, rhs, value.shape[1])
                    value = dot(wide_parents[block], maps[parity][side]).astype(BF16)
                    first = block * parents + side * parents // 2
                    value = value.reshape(parents // 2, rhs, value.shape[1])
                    parent_table[first : first + parents // 2, rows, :] = value

        own[6].wait()

        def some_leaves(step, carry):
            for inner in range(8):
                leaf = step * 8 + inner
                product = dot(collect(moment_table, lambda row, link: far_leaf[link, row], leaf, me * leaves), leaf_couplings[leaf])
                far[pl.ds(pl.multiple_of(leaf * rhs, rhs), rhs), :] = fold(product, rhs, rank)
            return carry

        lax.fori_loop(0, leaves // 8, some_leaves, 0)

    for index in range(9, 13):
        own[index].wait()
    lax.fori_loop(0, SPLIT, own_near, 0)
    for step in range(1, along):
        from_row(step).wait_send()
        from_row(step).wait_recv()
    in_row[column] = moment
    couplings = []
    value = in_row[...].reshape(along * rhs, rank)
    nodes = along
    while nodes > 1:
        value = tree_level(value, column // (along // nodes), nodes, couplings)
        nodes = nodes // 2
    sent[1] = value
    for step in range(1, across):
        to_column(step).start()
    send((4,))
    lax.fori_loop(SPLIT, leaves // batch, own_near, 0)
    for step in range(1, across):
        from_column(step).wait_send()
        from_column(step).wait_recv()
    in_column[row] = value
    value = in_column[...].reshape(across * rhs, rank)
    nodes = across
    while nodes > 1:
        value = tree_level(value, row // (across // nodes), nodes, couplings)
        nodes = nodes // 2
    far_leaves()
    _, field = couplings[-1]
    for side, coupling in reversed(couplings[:-1]):
        field = coupling + ROOT_TWO * dot(field.astype(BF16), top_transfer[side], 1, 1)
    device_local = field.astype(BF16).astype(F32)

    own[5].wait()
    down = spread_down(device_local, parent_maps[...], plain, mask, links, rhs)
    parent_local = []
    for parent in range(parents):
        product = dot(collect(parent_table, lambda row, link: far_cluster[row, link], parent, me * parents), parent_couplings[parent])
        value = fold(product, rhs, rank) + down[parent * rhs : (parent + 1) * rhs]
        parent_local.append(value.astype(BF16).astype(F32))
    for parent in range(parents):
        down = spread_down(parent_local[parent], leaf_maps[parent], plain, mask, links, rhs)
        rows = slice(parent * links * rhs, (parent + 1) * links * rhs)
        local[rows, :] = (far[rows, :] + down).astype(BF16)

    def finish(step, carry):
        for inner in range(8):
            leaf = step * 8 + inner
            value = local[pl.ds(pl.multiple_of(leaf * rhs, rhs), rhs), :]
            partial[leaf] = partial[leaf] + dot(value, basis[leaf])
        return carry

    lax.fori_loop(0, leaves // 8, finish, 0)
    result = pltpu.make_async_copy(partial, partial_hbm, own_sem.at[len(own)])
    result.start()
    settle((0, 1, 4))
    result.wait()
    keep.wait()


def near_kernel(
    pairs,
    points_hbm,
    charges_hbm,
    side_points_hbm,
    side_charges_hbm,
    partial_hbm,
    columns_hbm,
    potential,
    points,
    charges,
    source_points,
    columns,
    sem,
):
    leaves, rhs, size = potential.shape
    tail = pairs.shape[1] - 128
    count = pairs[0, tail + QUARTERS]
    span = leaves // QUARTERS
    steps = [(columns_hbm.at[pl.ds(at, span)], columns.at[pl.ds(at, span)]) for at in range(0, leaves, span)]
    moves = [
        (points_hbm, points.at[2]),
        (side_points_hbm, points.at[pl.ds(0, 2)]),
        steps[0],
        (side_charges_hbm.at[0], charges.at[pl.ds(0, leaves)]),
        (side_charges_hbm.at[1], charges.at[pl.ds(leaves, leaves)]),
        (charges_hbm, charges.at[pl.ds(2 * leaves, leaves)]),
        (partial_hbm, potential),
    ] + steps[1:]
    copies = [
        pltpu.make_async_copy(source, target, sem.at[index]) for index, (source, target) in enumerate(moves)
    ]
    for copy in copies:
        copy.start()
    copies[0].wait()
    copies[1].wait()
    for block in range(3):
        put_points(source_points, points.at[block], block * leaves)
    for copy in copies[2:7]:
        copy.wait()

    def some_pairs(step, carry):
        results = []
        for inner in range(GROUP):
            at = step * GROUP + inner
            code = pairs[0, at]
            source = code // leaves
            target = code % leaves
            value = near_value(columns, target, source_points, [source], [charges[source]])
            results.append((target, jnp.where(at < count, value, 0.0)))
        for target, value in results:
            potential[target] = potential[target] + value
        return carry

    done = 0
    for quarter in range(QUARTERS):
        if quarter > 0:
            copies[6 + quarter].wait()
        bound = pairs[0, tail + 1 + quarter] // GROUP if quarter < QUARTERS - 1 else (count + GROUP - 1) // GROUP
        lax.fori_loop(done, bound, some_pairs, 0)
        done = bound


def stored(matrix, links):
    length = matrix.shape[-1]
    tiles = length // 128
    value = matrix.reshape(-1, links, tiles, 128).transpose(0, 2, 1, 3)
    return value.reshape(-1, tiles * links, 128)


def on_device(
    grid_shape,
    points,
    charges,
    near_list,
    near_count,
    far_leaf,
    far_cluster,
    basis,
    leaf_transfer,
    cluster_transfer,
    leaf_coupling,
    cluster_coupling,
    top_transfer,
    top_coupling,
):
    leaves, rhs, size = charges.shape
    rank = basis.shape[1]
    parents = cluster_transfer.shape[0]
    links = far_leaf.shape[1]
    slots = near_list.shape[1]
    across, along = grid_shape
    turned = points.transpose(1, 0, 2)
    leaf_maps = stored(leaf_transfer, links)
    parent_maps = stored(cluster_transfer, links)[0]
    leaf_couplings = stored(leaf_coupling, links)
    parent_couplings = stored(cluster_coupling, links)
    hbm = pl.BlockSpec(memory_space=pl.ANY)
    shape = jax.ShapeDtypeStruct
    spread = rank // 2 * links
    length = slots * leaves + 2 * 128
    count_row = near_count.reshape(1, leaves)
    pairs, side_points, side_charges, partial, columns = pl.pallas_call(
        functools.partial(exchange_kernel, grid_shape),
        out_shape=(
            shape((1, length), jnp.int32),
            shape((2,) + turned.shape, BF16),
            shape((2,) + charges.shape, BF16),
            shape((leaves, rhs, size), F32),
            shape((leaves, 3, size, 128), BF16),
        ),
        in_specs=[hbm] * 13,
        out_specs=(pl.BlockSpec(memory_space=pltpu.VMEM), hbm, hbm, hbm, hbm),
        scratch_shapes=[
            pltpu.SMEM((links, leaves), jnp.int32),
            pltpu.SMEM((parents, links), jnp.int32),
            pltpu.VMEM((slots, leaves), jnp.int32),
            pltpu.VMEM((1, leaves), jnp.int32),
            pltpu.VMEM(top_transfer.shape, BF16),
            pltpu.VMEM(top_coupling.shape, BF16),
            pltpu.VMEM((leaves, rhs, size), F32),
            pltpu.VMEM((leaves + 1, 8, size), F32),
            pltpu.VMEM((leaves, 3, size, 128), BF16),
            pltpu.VMEM(turned.shape, BF16),
            pltpu.VMEM((3, leaves // 2 * rhs, 2 * rank), BF16),
            pltpu.VMEM((3, parents // 2 * rhs, 2 * rank), BF16),
            pltpu.VMEM((leaves + 1, rhs, size), BF16),
            pltpu.VMEM(basis.shape, BF16),
            pltpu.VMEM(leaf_maps.shape, BF16),
            pltpu.VMEM(parent_maps.shape, BF16),
            pltpu.VMEM(parent_couplings.shape, BF16),
            pltpu.VMEM(leaf_couplings.shape, BF16),
            pltpu.VMEM((3 * leaves, 2 * rhs, spread), BF16),
            pltpu.VMEM((3 * parents, 2 * rhs, spread), BF16),
            pltpu.VMEM((leaves * rhs, rank), F32),
            pltpu.VMEM((leaves * rhs, rank), BF16),
            pltpu.VMEM((2, rhs, rank), BF16),
            pltpu.VMEM((along, rhs, rank), BF16),
            pltpu.VMEM((across, rhs, rank), BF16),
            pltpu.VMEM((max(along, across), rhs, rank), BF16),
            pltpu.VMEM((8, 128), jnp.int32),
            pltpu.SMEM((8, 128), jnp.int32),
            pltpu.SemaphoreType.DMA((5, 2)),
            pltpu.SemaphoreType.DMA((5, 2)),
            pltpu.SemaphoreType.DMA((along,)),
            pltpu.SemaphoreType.DMA((along,)),
            pltpu.SemaphoreType.DMA((across,)),
            pltpu.SemaphoreType.DMA((across,)),
            pltpu.SemaphoreType.DMA((15,)),
        ],
        compiler_params=pltpu.CompilerParams(
            collective_id=0, has_side_effects=True, vmem_limit_bytes=EXCHANGE_MIB << 20
        ),
        name="exchange",
    )(
        far_leaf.T,
        far_cluster,
        near_list.T,
        count_row,
        top_transfer,
        top_coupling,
        turned,
        charges,
        basis,
        leaf_maps,
        parent_maps,
        parent_couplings,
        leaf_couplings,
    )
    return pl.pallas_call(
        near_kernel,
        out_shape=shape((leaves, rhs, size), F32),
        in_specs=[pl.BlockSpec(memory_space=pltpu.SMEM)] + [hbm] * 6,
        out_specs=pl.BlockSpec(memory_space=pltpu.VMEM),
        scratch_shapes=[
            pltpu.VMEM((3,) + turned.shape, BF16),
            pltpu.VMEM((3 * leaves, rhs, size), BF16),
            pltpu.VMEM((3 * leaves, 8, size), F32),
            pltpu.VMEM((leaves, 3, size, 128), BF16),
            pltpu.SemaphoreType.DMA((6 + QUARTERS,)),
        ],
        compiler_params=pltpu.CompilerParams(vmem_limit_bytes=NEAR_MIB << 20),
        name="near",
    )(pairs, turned, charges, side_points, side_charges, partial, columns)


def solution(mesh):
    grid_shape = (mesh.shape["gx"], mesh.shape["gy"])
    both = ("gx", "gy")
    in_specs = (
        P(both, None, None),
        P(both, None, None),
        P(both, None),
        P(both),
        P(both, None),
        P(both, None),
        P(both, None, None),
        P(both, None),
        P(both, None),
        P(both, None, None),
        P(both, None, None),
        P(),
        P(),
    )
    return jax.shard_map(
        functools.partial(on_device, grid_shape),
        mesh=mesh,
        in_specs=in_specs,
        out_specs=P(both, None, None),
        check_vma=False,
    )
```

```python
import functools

import jax
import jax.numpy as jnp
from jax import lax
from jax.experimental import pallas as pl
from jax.experimental.pallas import tpu as pltpu
from jax.sharding import PartitionSpec as P

SOFTENING = 0.0025
ROOT_TWO = 1.4142135623730951
MESH = pl.DeviceIdType.MESH
F32 = jnp.float32
BF16 = jnp.bfloat16
SCALE = 16.0
EARLY = 3
MIDDLE = 48
FIRST = 8
SPLIT = 2
QUARTERS = 4
GROUP = 8
EXCHANGE_MIB = 60
NEAR_MIB = 60


def dot(a, b, left=1, right=0):
    return lax.dot_general(a, b, (((left,), (right,)), ((), ())), preferred_element_type=F32)


def spread_map(parity, rank, links, side):
    lane = lax.broadcasted_iota(jnp.int32, (2 * rank, rank // 2 * links), 1)
    row = lax.broadcasted_iota(jnp.int32, (2 * rank, rank // 2 * links), 0)
    return jnp.where(row == side * rank + lane // links * 2 + parity, 1.0, 0.0).astype(BF16)


def link_mask(rows, links, lanes, per_link):
    lane = lax.broadcasted_iota(jnp.int32, (rows, lanes), 1)
    row = lax.broadcasted_iota(jnp.int32, (rows, lanes), 0)
    return jnp.where(lane % links == row // per_link, 1.0, 0.0)


def fold(product, rhs, rank):
    return product[:rhs, :rank] + product[rhs:, rank:]


def gathered_up(spreads, mask, links, rhs):
    halves = []
    for spread in spreads:
        wide = spread * mask
        halves.append(wide.reshape(links, rhs, wide.shape[1]).sum(axis=0))
    return jnp.concatenate(halves, axis=0).astype(BF16)


def block_diagonal(value):
    zero = jnp.zeros_like(value)
    upper = jnp.concatenate([value, zero], axis=1)
    lower = jnp.concatenate([zero, value], axis=1)
    return jnp.concatenate([upper, lower], axis=0).astype(BF16)


def spread_down(value, matrix, maps, mask, links, rhs):
    product = dot(block_diagonal(value), matrix, 1, 1)
    total = None
    for parity, spread in enumerate(maps):
        half = product[parity * rhs : (parity + 1) * rhs]
        tall = (jnp.concatenate([half] * links, axis=0) * mask).astype(BF16)
        part = dot(tall, spread, 1, 1)
        total = part if total is None else total + part
    return total


def put_points(table, points, at):
    for start in range(0, points.shape[1], 16):
        for axis in range(3):
            rows = points[axis, start : start + 16, :].astype(F32) * SCALE
            table[at + start : at + start + 16, axis, :] = rows


def put_columns(columns, points, source, leaf):
    for axis in range(3):
        row = points[source, axis : axis + 1, :]
        columns[leaf, axis] = jnp.broadcast_to(row, (128, row.shape[1])).astype(BF16).T


def near_tiles(columns, leaf, points, sources):
    size = points.shape[2]
    softening = jnp.asarray(SOFTENING * SCALE * SCALE, BF16)
    sides = [
        [jnp.broadcast_to(points[source, axis : axis + 1, :], (16, size)).astype(BF16) for axis in range(3)]
        for source in sources
    ]
    parts = [[] for _ in sources]
    for start in range(0, size, 16):
        target = []
        for axis in range(3):
            column = columns[leaf, axis, start : start + 16, :]
            target.append(jnp.concatenate([column] * (size // 128), axis=1))
        for side, part in zip(sides, parts):
            squared = softening
            for axis in range(3):
                apart = target[axis] - side[axis]
                squared = squared + apart * apart
            part.append(lax.rsqrt(squared))
    return [jnp.concatenate(part, axis=0) for part in parts]


def near_value(columns, leaf, points, sources, charges):
    tiles = near_tiles(columns, leaf, points, sources)
    tile = jnp.concatenate(tiles, axis=1) if len(tiles) > 1 else tiles[0]
    value = jnp.concatenate(charges, axis=1) if len(charges) > 1 else charges[0]
    return dot(tile, value, 1, 1).T


def ramp(shape, axis):
    return lax.broadcasted_iota(jnp.int32, shape, axis)


def triangle(size):
    return jnp.where(ramp((size, size), 0) < ramp((size, size), 1), 1.0, 0.0).astype(BF16)


def order_of(chosen):
    slots, leaves = chosen.shape
    ones = jnp.where(chosen, 1.0, 0.0)
    per_leaf = jnp.broadcast_to(ones.sum(axis=0, keepdims=True), (8, leaves)).astype(BF16)
    before = dot(per_leaf, triangle(leaves)) + dot(triangle(slots), ones.astype(BF16), 0, 0)
    return per_leaf, jnp.where(chosen, before, -1.0)


def compacted(spot, code, length, count, empty):
    slots, leaves = spot.shape
    spot = spot.T
    code = code.astype(F32).T
    at = ramp((leaves, length), 1).astype(F32)
    found = jnp.zeros((leaves, length), F32)
    for index in range(slots):
        hit = spot[:, index : index + 1] == at
        found = found + jnp.where(hit, code[:, index : index + 1], 0.0)
    return jnp.where(at[:1] < count, found.sum(axis=0, keepdims=True), 1.0 * empty)


def plan(near_list, near_count, first, leaves):
    slots = near_list.shape[0]
    half = leaves // 2
    source = near_list - first
    slot = ramp((slots, leaves), 0)
    leaf = ramp((slots, leaves), 1)
    live = slot < near_count
    inside = live & (source >= 0) & (source < leaves)
    ones = jnp.where(inside, 1.0, 0.0).astype(BF16)
    rank_of = dot(triangle(slots), ones, 0, 0).astype(jnp.int32)
    chosen = []
    for place_at in range(EARLY):
        here = inside & (rank_of == place_at)
        picked = jnp.where(here, source - leaves, 0).sum(axis=0, keepdims=True) + leaves
        chosen.append(picked)
    later = live & jnp.logical_not(inside & (rank_of < EARLY))
    near = later & (source >= -half) & (source < leaves + half)
    per_leaf, spot = order_of(near)
    taken = near & (spot < 1.0 * MIDDLE)
    count = jnp.minimum(per_leaf.astype(F32).sum(axis=1, keepdims=True)[:1], 1.0 * MIDDLE)
    outside = jnp.where(source < 0, source + leaves + half + 1, source + half + 1)
    row = jnp.where((source >= 0) & (source < leaves), source, outside)
    middle = compacted(jnp.where(taken, spot, -1.0), row * leaves + leaf, 128, count, leaves * leaves)
    middle_count = jnp.broadcast_to(count, (1, 128))
    later = later & jnp.logical_not(taken)
    per_leaf, spot = order_of(later)
    quarter = jnp.where(ramp((leaves, 128), 0) < ramp((leaves, 128), 1) * (leaves // QUARTERS), 1.0, 0.0)
    tail = dot(per_leaf, quarter.astype(BF16))[:1]
    count = tail[:, QUARTERS : QUARTERS + 1]
    row = jnp.where(source < 0, source + leaves, jnp.where(source < leaves, source + 2 * leaves, source))
    empty = 2 * leaves * leaves
    pairs = compacted(spot, row * leaves + leaf, slots * leaves, count, empty)
    spare = jnp.full((1, 128), 1.0 * empty, F32)
    listed = jnp.concatenate([pairs, spare, middle, middle_count, tail], axis=1)
    return chosen, middle.astype(jnp.int32), listed.astype(jnp.int32)


def exchange_kernel(
    grid_shape,
    far_leaf_hbm,
    far_cluster_hbm,
    near_list_hbm,
    near_count_hbm,
    top_transfer_hbm,
    top_coupling_hbm,
    points_hbm,
    charges_hbm,
    basis_hbm,
    leaf_maps_hbm,
    parent_maps_hbm,
    parent_couplings_hbm,
    leaf_couplings_hbm,
    pairs,
    side_points,
    side_charges,
    partial_hbm,
    columns_hbm,
    extra_hbm,
    far_leaf,
    far_cluster,
    near_list,
    near_count,
    top_transfer,
    top_coupling,
    partial,
    source_points,
    columns,
    own_points,
    wide_moments,
    wide_parents,
    own_charges,
    basis,
    leaf_maps,
    parent_maps,
    parent_couplings,
    leaf_couplings,
    moment_table,
    parent_table,
    far,
    local,
    sent,
    in_row,
    in_column,
    tree,
    chosen,
    early_source,
    send_sem,
    recv_sem,
    row_send,
    row_recv,
    column_send,
    column_recv,
    own_sem,
    side_sem,
    near_points,
    extra,
):
    across, along = grid_shape
    total = across * along
    me = lax.axis_index("gx") * along + lax.axis_index("gy")
    leaves, rhs, size = partial.shape
    rank = basis.shape[1]
    parents = leaf_maps.shape[0]
    links = leaves // parents

    def place(index):
        return (index // along, index % along)

    barrier = pltpu.get_barrier_semaphore()

    row, column = lax.axis_index("gx"), lax.axis_index("gy")

    def beside(step):
        return (row, (column + step) % along)

    def across_from(step):
        return ((row + step) % across, column)

    for step in range(1, along):
        pl.semaphore_signal(barrier, inc=1, device_id=beside(step), device_id_type=MESH)
    for step in range(1, across):
        pl.semaphore_signal(barrier, inc=1, device_id=across_from(step), device_id_type=MESH)
    first_of_row = (column == 0) & (row > 0)
    last_of_row = (column == along - 1) & (row < across - 1)

    @pl.when(first_of_row)
    def _():
        pl.semaphore_signal(barrier, inc=1, device_id=(row - 1, along - 1), device_id_type=MESH)

    @pl.when(last_of_row)
    def _():
        pl.semaphore_signal(barrier, inc=1, device_id=(row + 1, 0), device_id_type=MESH)
    own = [
        pltpu.make_async_copy(source, target, own_sem.at[index])
        for index, (source, target) in enumerate(
            (
                (points_hbm, own_points),
                (charges_hbm, own_charges.at[pl.ds(0, leaves)]),
                (basis_hbm, basis),
                (leaf_maps_hbm, leaf_maps),
                (parent_maps_hbm, parent_maps),
                (parent_couplings_hbm, parent_couplings),
                (leaf_couplings_hbm, leaf_couplings),
                (near_list_hbm, near_list),
                (near_count_hbm, near_count),
                (far_leaf_hbm, far_leaf),
                (far_cluster_hbm, far_cluster),
                (top_transfer_hbm, top_transfer),
                (top_coupling_hbm, top_coupling),
            )
        )
    ]
    for copy in own:
        copy.start()

    moments_of = wide_moments.shape[1]
    half = leaves // 2

    cuts = (0, leaves // FIRST, half, leaves)

    def part_of(ref, side, part):
        low, high = cuts[part], cuts[part + 1]
        return ref.at[pl.ds(leaves - high if side == 0 else low, high - low)]

    def charge_parts(part):
        sources = [part_of(charges_hbm, side, part) for side in range(2)]
        return sources, [part_of(side_charges.at[side], side, part) for side in range(2)]

    flows = (
        charge_parts(0),
        ([points_hbm] * 2, [side_points.at[side] for side in range(2)]),
        ([wide_parents.at[2]] * 2, [wide_parents.at[side] for side in range(2)]),
        ([wide_moments.at[2]] * 2, [wide_moments.at[side] for side in range(2)]),
        charge_parts(1),
        charge_parts(2),
    )

    def rightward(index):
        return pltpu.make_async_remote_copy(
            src_ref=flows[index][0][0],
            dst_ref=flows[index][1][0],
            send_sem=send_sem.at[index, 0],
            recv_sem=recv_sem.at[index, 0],
            device_id=place(jnp.minimum(me + 1, total - 1)),
            device_id_type=MESH,
        )

    def leftward(index):
        return pltpu.make_async_remote_copy(
            src_ref=flows[index][0][1],
            dst_ref=flows[index][1][1],
            send_sem=send_sem.at[index, 1],
            recv_sem=recv_sem.at[index, 1],
            device_id=place(jnp.maximum(me - 1, 0)),
            device_id_type=MESH,
        )

    def to_row(step):
        return pltpu.make_async_remote_copy(
            src_ref=sent.at[0],
            dst_ref=in_row.at[column],
            send_sem=row_send.at[step],
            recv_sem=row_recv.at[column],
            device_id=beside(step),
            device_id_type=MESH,
        )

    def from_row(step):
        source = (column + step) % along
        return pltpu.make_async_remote_copy(
            src_ref=sent.at[0],
            dst_ref=in_row.at[source],
            send_sem=row_send.at[step],
            recv_sem=row_recv.at[source],
            device_id=beside(step),
            device_id_type=MESH,
        )

    def to_column(step):
        return pltpu.make_async_remote_copy(
            src_ref=sent.at[1],
            dst_ref=in_column.at[row],
            send_sem=column_send.at[step],
            recv_sem=column_recv.at[row],
            device_id=across_from(step),
            device_id_type=MESH,
        )

    def from_column(step):
        source = (row + step) % across
        return pltpu.make_async_remote_copy(
            src_ref=sent.at[1],
            dst_ref=in_column.at[source],
            send_sem=column_send.at[step],
            recv_sem=column_recv.at[source],
            device_id=across_from(step),
            device_id_type=MESH,
        )

    def tree_level(value, index, nodes, couple):
        side = index % 2
        tree[:nodes] = value.reshape(nodes, rhs, rank)
        couple.append((side, dot(tree[index + 1 - 2 * side], top_coupling[side])))
        pair = value.reshape(nodes // 2, 2 * rhs, rank)
        lower = pair[:, :rhs].reshape(nodes // 2 * rhs, rank)
        upper = pair[:, rhs:].reshape(nodes // 2 * rhs, rank)
        return (dot(lower, top_transfer[0]) + dot(upper, top_transfer[1])).astype(BF16)

    def send(indices):
        @pl.when(me < total - 1)
        def _():
            for index in indices:
                rightward(index).start()

        @pl.when(me > 0)
        def _():
            for index in indices:
                leftward(index).start()

    def settle(indices):
        @pl.when(me < total - 1)
        def _():
            for index in indices:
                rightward(index).wait_send()
                leftward(index).wait_recv()

        @pl.when(me > 0)
        def _():
            for index in indices:
                leftward(index).wait_send()
                rightward(index).wait_recv()

    corners = jnp.where(first_of_row | last_of_row, 1, 0)
    pl.semaphore_wait(barrier, along + across - 2 + corners)
    send((1, 0))

    maps = [[spread_map(parity, rank, links, side) for side in range(2)] for parity in range(2)]
    plain = [spread_map(parity, rank, links, 0)[:rank] for parity in range(2)]
    lanes = rank // 2 * links
    mask = link_mask(links * rhs, links, lanes, rhs)
    lane = lax.broadcasted_iota(jnp.int32, (2 * rhs, lanes), 1) % links
    masks = [jnp.where(lane == link, 1.0, 0.0).astype(BF16) for link in range(links)]

    own[1].wait()
    own[2].wait()
    group = 4

    def one_moment(step, carry):
        for inner in range(group):
            leaf = step * group + inner
            pair = [dot(own_charges[at], basis[at], 1, 1) for at in (leaf, leaf + half)]
            value = jnp.concatenate(pair, axis=1).astype(BF16)
            wide_moments[2, pl.ds(pl.multiple_of(leaf * rhs, rhs), rhs), :] = value
        return carry

    lax.fori_loop(0, half // group, one_moment, 0)
    own[3].wait()
    raised = []
    for parent in range(parents):
        first = parent * links * rhs % moments_of
        stack = wide_moments[2, first : first + links * rhs, :]
        wide = [dot(stack, maps[parity][parent * links // half]) for parity in range(2)]
        product = dot(gathered_up(wide, mask, links, rhs), leaf_maps[parent])
        raised.append(fold(product, rhs, rank))
    for parent in range(parents // 2):
        value = jnp.concatenate([raised[parent], raised[parent + parents // 2]], axis=1).astype(BF16)
        wide_parents[2, parent * rhs : (parent + 1) * rhs, :] = value
    own[4].wait()
    stack = wide_parents[2]
    wide = [jnp.concatenate([dot(stack, side) for side in sides], axis=0) for sides in maps]
    product = dot(gathered_up(wide, mask, parents, rhs), parent_maps[...])
    moment = fold(product, rhs, rank).astype(BF16)
    sent[0] = moment
    for step in range(1, along):
        to_row(step).start()
    send((2, 3))

    @pl.when(me == 0)
    def _():
        wide_moments[0] = jnp.zeros(wide_moments.shape[1:], BF16)
        wide_parents[0] = jnp.zeros(wide_parents.shape[1:], BF16)

    @pl.when(me == total - 1)
    def _():
        wide_moments[1] = jnp.zeros(wide_moments.shape[1:], BF16)
        wide_parents[1] = jnp.zeros(wide_parents.shape[1:], BF16)

    own[7].wait()
    own[8].wait()
    picked, middle, listed = plan(near_list[...], near_count[...], me * leaves, leaves)
    pairs[...] = listed
    for index, value in enumerate(picked):
        chosen[index : index + 1, :leaves] = value
    chosen[EARLY : EARLY + 1, :] = middle
    choose = pltpu.make_async_copy(chosen, early_source, own_sem.at[len(own)])
    choose.start()

    own_charges[leaves] = jnp.zeros((rhs, size), BF16)
    own[0].wait()
    put_points(source_points, own_points, 0)
    source_points[leaves] = jnp.zeros(source_points.shape[1:], F32)

    def one_column(step, carry):
        for inner in range(group):
            leaf = step * group + inner
            put_columns(columns, source_points, leaf, leaf)
        return carry

    lax.fori_loop(0, leaves // group, one_column, 0)
    keep = pltpu.make_async_copy(columns, columns_hbm, own_sem.at[len(own) + 1])
    keep.start()
    choose.wait()
    batch = 4

    def own_near(step, carry):
        results = []
        for inner in range(batch):
            leaf = step * batch + inner
            found = [early_source[index, leaf] for index in range(EARLY)]
            charges = [own_charges[source] for source in found]
            results.append(near_value(columns, leaf, source_points, found, charges))
        for inner in range(batch):
            partial[step * batch + inner] = results[inner]
        return carry

    def collect(table, index, row, first):
        gathered = None
        for link in range(links):
            source = index(row, link) - first
            span = table.shape[0] // 3
            at = jnp.where(source < 0, source + span, jnp.where(source < span, source + 2 * span, source))
            at = jnp.clip(at, 0, table.shape[0] - 1)
            part = table[at] * masks[link]
            gathered = part if gathered is None else gathered + part
        return gathered

    def far_leaves():
        settle((2, 3))
        for block in range(3):
            for parity in range(2):
                for side in range(2):
                    value = dot(wide_moments[block], maps[parity][side]).astype(BF16)
                    first = block * leaves + side * half
                    rows = slice(parity * rhs, (parity + 1) * rhs)
                    moment_table[first : first + half, rows, :] = value.reshape(half, rhs, value.shape[1])
                    value = dot(wide_parents[block], maps[parity][side]).astype(BF16)
                    first = block * parents + side * parents // 2
                    value = value.reshape(parents // 2, rhs, value.shape[1])
                    parent_table[first : first + parents // 2, rows, :] = value

        own[6].wait()

        def some_leaves(step, carry):
            for inner in range(8):
                leaf = step * 8 + inner
                product = dot(collect(moment_table, lambda row, link: far_leaf[link, row], leaf, me * leaves), leaf_couplings[leaf])
                far[pl.ds(pl.multiple_of(leaf * rhs, rhs), rhs), :] = fold(product, rhs, rank)
            return carry

        lax.fori_loop(0, leaves // 8, some_leaves, 0)

    for index in range(9, 13):
        own[index].wait()
    lax.fori_loop(0, SPLIT, own_near, 0)
    for step in range(1, along):
        from_row(step).wait_send()
        from_row(step).wait_recv()
    in_row[column] = moment
    couplings = []
    value = in_row[...].reshape(along * rhs, rank)
    nodes = along
    while nodes > 1:
        value = tree_level(value, column // (along // nodes), nodes, couplings)
        nodes = nodes // 2
    sent[1] = value
    for step in range(1, across):
        to_column(step).start()
    send((4,))
    lax.fori_loop(SPLIT, leaves // batch, own_near, 0)
    for step in range(1, across):
        from_column(step).wait_send()
        from_column(step).wait_recv()
    in_column[row] = value
    value = in_column[...].reshape(across * rhs, rank)
    nodes = across
    while nodes > 1:
        value = tree_level(value, row // (across // nodes), nodes, couplings)
        nodes = nodes // 2
    send((5,))
    far_leaves()
    _, field = couplings[-1]
    for side, coupling in reversed(couplings[:-1]):
        field = coupling + ROOT_TWO * dot(field.astype(BF16), top_transfer[side], 1, 1)
    device_local = field.astype(BF16).astype(F32)

    own[5].wait()
    down = spread_down(device_local, parent_maps[...], plain, mask, links, rhs)
    parent_local = []
    for parent in range(parents):
        product = dot(collect(parent_table, lambda row, link: far_cluster[row, link], parent, me * parents), parent_couplings[parent])
        value = fold(product, rhs, rank) + down[parent * rhs : (parent + 1) * rhs]
        parent_local.append(value.astype(BF16).astype(F32))
    for parent in range(parents):
        down = spread_down(parent_local[parent], leaf_maps[parent], plain, mask, links, rhs)
        rows = slice(parent * links * rhs, (parent + 1) * links * rhs)
        local[rows, :] = (far[rows, :] + down).astype(BF16)

    def finish(step, carry):
        for inner in range(8):
            leaf = step * 8 + inner
            value = local[pl.ds(pl.multiple_of(leaf * rhs, rhs), rhs), :]
            partial[leaf] = partial[leaf] + dot(value, basis[leaf])
        return carry

    settle((1, 0, 4))

    def near_side(side):
        rows = pl.ds(leaves - half if side == 0 else 0, half)
        held = pl.ds(leaves + 1 + side * half, half)
        return (
            pltpu.make_async_copy(side_charges.at[side, rows], own_charges.at[held], side_sem.at[side, 0]),
            pltpu.make_async_copy(side_points.at[side], near_points.at[side], side_sem.at[side, 1]),
        )

    @pl.when(me > 0)
    def _():
        for copy in near_side(0):
            copy.start()

    @pl.when(me < total - 1)
    def _():
        for copy in near_side(1):
            copy.start()

    lax.fori_loop(0, leaves // 8, finish, 0)
    result = pltpu.make_async_copy(partial, partial_hbm, own_sem.at[len(own)])
    result.start()

    @pl.when(me > 0)
    def _():
        for copy in near_side(0):
            copy.wait()
        put_points(source_points, near_points.at[0, :, leaves - half :], leaves + 1)

    @pl.when(me < total - 1)
    def _():
        for copy in near_side(1):
            copy.wait()
        put_points(source_points, near_points.at[1, :, :half], leaves + 1 + half)

    def some_middle(step, carry):
        results = []
        for inner in range(GROUP):
            code = jnp.clip(early_source[EARLY, step * GROUP + inner], 0, (2 * leaves + 1) * leaves - 1)
            source = code // leaves
            results.append(near_value(columns, code % leaves, source_points, [source], [own_charges[source]]))
        for inner in range(GROUP):
            extra[step * GROUP + inner] = results[inner]
        return carry

    halfway = MIDDLE // GROUP // 2
    moved = []
    for index, (low, high) in enumerate(((0, halfway), (halfway, MIDDLE // GROUP))):
        lax.fori_loop(low, high, some_middle, 0)
        rows = pl.ds(low * GROUP, (high - low) * GROUP)
        move = pltpu.make_async_copy(extra.at[rows], extra_hbm.at[rows], own_sem.at[len(own) + 2 + index])
        move.start()
        moved.append(move)
    settle((5,))
    for move in moved:
        move.wait()
    result.wait()
    keep.wait()


def near_kernel(
    pairs,
    points_hbm,
    charges_hbm,
    side_points_hbm,
    side_charges_hbm,
    partial_hbm,
    columns_hbm,
    extra_hbm,
    potential,
    points,
    charges,
    source_points,
    columns,
    extra,
    sem,
):
    leaves, rhs, size = potential.shape
    tail = pairs.shape[1] - 128
    count = pairs[0, tail + QUARTERS]
    span = leaves // QUARTERS
    steps = [(columns_hbm.at[pl.ds(at, span)], columns.at[pl.ds(at, span)]) for at in range(0, leaves, span)]
    moves = [
        (points_hbm, points.at[2]),
        (side_points_hbm, points.at[pl.ds(0, 2)]),
        (partial_hbm, potential),
        (extra_hbm, extra),
        steps[0],
        (side_charges_hbm.at[0], charges.at[pl.ds(0, leaves)]),
        (side_charges_hbm.at[1], charges.at[pl.ds(leaves, leaves)]),
        (charges_hbm, charges.at[pl.ds(2 * leaves, leaves)]),
    ] + steps[1:]
    copies = [
        pltpu.make_async_copy(source, target, sem.at[index]) for index, (source, target) in enumerate(moves)
    ]
    for copy in copies:
        copy.start()
    copies[0].wait()
    copies[1].wait()
    for block in range(3):
        put_points(source_points, points.at[block], block * leaves)
    copies[2].wait()
    copies[3].wait()

    def one_extra(index, carry):
        target = pairs[0, tail - 256 + index] % leaves
        potential[target] = potential[target] + extra[index]
        return carry

    lax.fori_loop(0, pairs[0, tail - 128], one_extra, 0)
    for copy in copies[4:8]:
        copy.wait()

    def some_pairs(step, carry):
        results = []
        for inner in range(GROUP):
            at = step * GROUP + inner
            code = pairs[0, at]
            source = code // leaves
            target = code % leaves
            value = near_value(columns, target, source_points, [source], [charges[source]])
            results.append((target, jnp.where(at < count, value, 0.0)))
        for target, value in results:
            potential[target] = potential[target] + value
        return carry

    done = 0
    for quarter in range(QUARTERS):
        if quarter > 0:
            copies[7 + quarter].wait()
        bound = pairs[0, tail + 1 + quarter] // GROUP if quarter < QUARTERS - 1 else (count + GROUP - 1) // GROUP
        lax.fori_loop(done, bound, some_pairs, 0)
        done = bound


def stored(matrix, links):
    length = matrix.shape[-1]
    tiles = length // 128
    value = matrix.reshape(-1, links, tiles, 128).transpose(0, 2, 1, 3)
    return value.reshape(-1, tiles * links, 128)


def on_device(
    grid_shape,
    points,
    charges,
    near_list,
    near_count,
    far_leaf,
    far_cluster,
    basis,
    leaf_transfer,
    cluster_transfer,
    leaf_coupling,
    cluster_coupling,
    top_transfer,
    top_coupling,
):
    leaves, rhs, size = charges.shape
    rank = basis.shape[1]
    parents = cluster_transfer.shape[0]
    links = far_leaf.shape[1]
    slots = near_list.shape[1]
    across, along = grid_shape
    turned = points.transpose(1, 0, 2)
    leaf_maps = stored(leaf_transfer, links)
    parent_maps = stored(cluster_transfer, links)[0]
    leaf_couplings = stored(leaf_coupling, links)
    parent_couplings = stored(cluster_coupling, links)
    hbm = pl.BlockSpec(memory_space=pl.ANY)
    shape = jax.ShapeDtypeStruct
    spread = rank // 2 * links
    length = slots * leaves + 4 * 128
    count_row = near_count.reshape(1, leaves)
    pairs, side_points, side_charges, partial, columns, extra = pl.pallas_call(
        functools.partial(exchange_kernel, grid_shape),
        out_shape=(
            shape((1, length), jnp.int32),
            shape((2,) + turned.shape, BF16),
            shape((2,) + charges.shape, BF16),
            shape((leaves, rhs, size), F32),
            shape((leaves, 3, size, 128), BF16),
            shape((MIDDLE, rhs, size), F32),
        ),
        in_specs=[hbm] * 13,
        out_specs=(pl.BlockSpec(memory_space=pltpu.VMEM), hbm, hbm, hbm, hbm, hbm),
        scratch_shapes=[
            pltpu.SMEM((links, leaves), jnp.int32),
            pltpu.SMEM((parents, links), jnp.int32),
            pltpu.VMEM((slots, leaves), jnp.int32),
            pltpu.VMEM((1, leaves), jnp.int32),
            pltpu.VMEM(top_transfer.shape, BF16),
            pltpu.VMEM(top_coupling.shape, BF16),
            pltpu.VMEM((leaves, rhs, size), F32),
            pltpu.VMEM((2 * leaves + 1, 8, size), F32),
            pltpu.VMEM((leaves, 3, size, 128), BF16),
            pltpu.VMEM(turned.shape, BF16),
            pltpu.VMEM((3, leaves // 2 * rhs, 2 * rank), BF16),
            pltpu.VMEM((3, parents // 2 * rhs, 2 * rank), BF16),
            pltpu.VMEM((2 * leaves + 1, rhs, size), BF16),
            pltpu.VMEM(basis.shape, BF16),
            pltpu.VMEM(leaf_maps.shape, BF16),
            pltpu.VMEM(parent_maps.shape, BF16),
            pltpu.VMEM(parent_couplings.shape, BF16),
            pltpu.VMEM(leaf_couplings.shape, BF16),
            pltpu.VMEM((3 * leaves, 2 * rhs, spread), BF16),
            pltpu.VMEM((3 * parents, 2 * rhs, spread), BF16),
            pltpu.VMEM((leaves * rhs, rank), F32),
            pltpu.VMEM((leaves * rhs, rank), BF16),
            pltpu.VMEM((2, rhs, rank), BF16),
            pltpu.VMEM((along, rhs, rank), BF16),
            pltpu.VMEM((across, rhs, rank), BF16),
            pltpu.VMEM((max(along, across), rhs, rank), BF16),
            pltpu.VMEM((8, 128), jnp.int32),
            pltpu.SMEM((8, 128), jnp.int32),
            pltpu.SemaphoreType.DMA((6, 2)),
            pltpu.SemaphoreType.DMA((6, 2)),
            pltpu.SemaphoreType.DMA((along,)),
            pltpu.SemaphoreType.DMA((along,)),
            pltpu.SemaphoreType.DMA((across,)),
            pltpu.SemaphoreType.DMA((across,)),
            pltpu.SemaphoreType.DMA((17,)),
            pltpu.SemaphoreType.DMA((2, 2)),
            pltpu.VMEM((2,) + turned.shape, BF16),
            pltpu.VMEM((MIDDLE, rhs, size), F32),
        ],
        compiler_params=pltpu.CompilerParams(
            collective_id=0, has_side_effects=True, vmem_limit_bytes=EXCHANGE_MIB << 20
        ),
        name="exchange",
    )(
        far_leaf.T,
        far_cluster,
        near_list.T,
        count_row,
        top_transfer,
        top_coupling,
        turned,
        charges,
        basis,
        leaf_maps,
        parent_maps,
        parent_couplings,
        leaf_couplings,
    )
    return pl.pallas_call(
        near_kernel,
        out_shape=shape((leaves, rhs, size), F32),
        in_specs=[pl.BlockSpec(memory_space=pltpu.SMEM)] + [hbm] * 7,
        out_specs=pl.BlockSpec(memory_space=pltpu.VMEM),
        scratch_shapes=[
            pltpu.VMEM((3,) + turned.shape, BF16),
            pltpu.VMEM((3 * leaves, rhs, size), BF16),
            pltpu.VMEM((3 * leaves, 8, size), F32),
            pltpu.VMEM((leaves, 3, size, 128), BF16),
            pltpu.VMEM((MIDDLE, rhs, size), F32),
            pltpu.SemaphoreType.DMA((7 + QUARTERS,)),
        ],
        compiler_params=pltpu.CompilerParams(vmem_limit_bytes=NEAR_MIB << 20),
        name="near",
    )(pairs, turned, charges, side_points, side_charges, partial, columns, extra)


def solution(mesh):
    grid_shape = (mesh.shape["gx"], mesh.shape["gy"])
    both = ("gx", "gy")
    in_specs = (
        P(both, None, None),
        P(both, None, None),
        P(both, None),
        P(both),
        P(both, None),
        P(both, None),
        P(both, None, None),
        P(both, None),
        P(both, None),
        P(both, None, None),
        P(both, None, None),
        P(),
        P(),
    )
    return jax.shard_map(
        functools.partial(on_device, grid_shape),
        mesh=mesh,
        in_specs=in_specs,
        out_specs=P(both, None, None),
        check_vma=False,
    )
```

```python
import functools

import jax
import jax.numpy as jnp
from jax import lax
from jax.experimental import pallas as pl
from jax.experimental.pallas import tpu as pltpu
from jax.sharding import PartitionSpec as P

SOFTENING = 0.0025
ROOT_TWO = 1.4142135623730951
MESH = pl.DeviceIdType.MESH
F32 = jnp.float32
BF16 = jnp.bfloat16
SCALE = 16.0
EARLY = 3
MIDDLE = 48
FIRST = 16
SPLIT = 4
QUARTERS = 4
GROUP = 8
EXCHANGE_MIB = 60
NEAR_MIB = 60


def dot(a, b, left=1, right=0):
    return lax.dot_general(a, b, (((left,), (right,)), ((), ())), preferred_element_type=F32)


def spread_map(parity, rank, links, side):
    lane = lax.broadcasted_iota(jnp.int32, (2 * rank, rank // 2 * links), 1)
    row = lax.broadcasted_iota(jnp.int32, (2 * rank, rank // 2 * links), 0)
    return jnp.where(row == side * rank + lane // links * 2 + parity, 1.0, 0.0).astype(BF16)


def link_mask(rows, links, lanes, per_link):
    lane = lax.broadcasted_iota(jnp.int32, (rows, lanes), 1)
    row = lax.broadcasted_iota(jnp.int32, (rows, lanes), 0)
    return jnp.where(lane % links == row // per_link, 1.0, 0.0)


def fold(product, rhs, rank):
    return product[:rhs, :rank] + product[rhs:, rank:]


def gathered_up(spreads, mask, links, rhs):
    halves = []
    for spread in spreads:
        wide = spread * mask
        halves.append(wide.reshape(links, rhs, wide.shape[1]).sum(axis=0))
    return jnp.concatenate(halves, axis=0).astype(BF16)


def block_diagonal(value):
    zero = jnp.zeros_like(value)
    upper = jnp.concatenate([value, zero], axis=1)
    lower = jnp.concatenate([zero, value], axis=1)
    return jnp.concatenate([upper, lower], axis=0).astype(BF16)


def spread_down(value, matrix, maps, mask, links, rhs):
    product = dot(block_diagonal(value), matrix, 1, 1)
    total = None
    for parity, spread in enumerate(maps):
        half = product[parity * rhs : (parity + 1) * rhs]
        tall = (jnp.concatenate([half] * links, axis=0) * mask).astype(BF16)
        part = dot(tall, spread, 1, 1)
        total = part if total is None else total + part
    return total


def put_points(table, points, at):
    for start in range(0, points.shape[1], 16):
        for axis in range(3):
            rows = points[axis, start : start + 16, :].astype(F32) * SCALE
            table[at + start : at + start + 16, axis, :] = rows


def put_columns(columns, points, source, leaf):
    for axis in range(3):
        row = points[source, axis : axis + 1, :]
        columns[leaf, axis] = jnp.broadcast_to(row, (128, row.shape[1])).astype(BF16).T


def near_tiles(columns, leaf, points, sources):
    size = points.shape[2]
    softening = jnp.asarray(SOFTENING * SCALE * SCALE, BF16)
    sides = [
        [jnp.broadcast_to(points[source, axis : axis + 1, :], (16, size)).astype(BF16) for axis in range(3)]
        for source in sources
    ]
    parts = [[] for _ in sources]
    for start in range(0, size, 16):
        target = []
        for axis in range(3):
            column = columns[leaf, axis, start : start + 16, :]
            target.append(jnp.concatenate([column] * (size // 128), axis=1))
        for side, part in zip(sides, parts):
            squared = softening
            for axis in range(3):
                apart = target[axis] - side[axis]
                squared = squared + apart * apart
            part.append(lax.rsqrt(squared))
    return [jnp.concatenate(part, axis=0) for part in parts]


def near_value(columns, leaf, points, sources, charges):
    tiles = near_tiles(columns, leaf, points, sources)
    tile = jnp.concatenate(tiles, axis=1) if len(tiles) > 1 else tiles[0]
    value = jnp.concatenate(charges, axis=1) if len(charges) > 1 else charges[0]
    return dot(tile, value, 1, 1).T


def ramp(shape, axis):
    return lax.broadcasted_iota(jnp.int32, shape, axis)


def triangle(size):
    return jnp.where(ramp((size, size), 0) < ramp((size, size), 1), 1.0, 0.0).astype(BF16)


def order_of(chosen):
    slots, leaves = chosen.shape
    ones = jnp.where(chosen, 1.0, 0.0)
    per_leaf = jnp.broadcast_to(ones.sum(axis=0, keepdims=True), (8, leaves)).astype(BF16)
    before = dot(per_leaf, triangle(leaves)) + dot(triangle(slots), ones.astype(BF16), 0, 0)
    return per_leaf, jnp.where(chosen, before, -1.0)


def compacted(spot, code, length, count, empty):
    slots, leaves = spot.shape
    spot = spot.T
    code = code.astype(F32).T
    at = ramp((leaves, length), 1).astype(F32)
    found = jnp.zeros((leaves, length), F32)
    for index in range(slots):
        hit = spot[:, index : index + 1] == at
        found = found + jnp.where(hit, code[:, index : index + 1], 0.0)
    return jnp.where(at[:1] < count, found.sum(axis=0, keepdims=True), 1.0 * empty)


def plan(near_list, near_count, first, leaves):
    slots = near_list.shape[0]
    half = leaves // 2
    source = near_list - first
    slot = ramp((slots, leaves), 0)
    leaf = ramp((slots, leaves), 1)
    live = slot < near_count
    inside = live & (source >= 0) & (source < leaves)
    ones = jnp.where(inside, 1.0, 0.0).astype(BF16)
    rank_of = dot(triangle(slots), ones, 0, 0).astype(jnp.int32)
    chosen = []
    for place_at in range(EARLY):
        here = inside & (rank_of == place_at)
        picked = jnp.where(here, source - leaves, 0).sum(axis=0, keepdims=True) + leaves
        chosen.append(picked)
    later = live & jnp.logical_not(inside & (rank_of < EARLY))
    near = later & (source >= -half) & (source < leaves + half)
    per_leaf, spot = order_of(near)
    taken = near & (spot < 1.0 * MIDDLE)
    count = jnp.minimum(per_leaf.astype(F32).sum(axis=1, keepdims=True)[:1], 1.0 * MIDDLE)
    outside = jnp.where(source < 0, source + leaves + half + 1, source + half + 1)
    row = jnp.where((source >= 0) & (source < leaves), source, outside)
    middle = compacted(jnp.where(taken, spot, -1.0), row * leaves + leaf, 128, count, leaves * leaves)
    middle_count = jnp.broadcast_to(count, (1, 128))
    later = later & jnp.logical_not(taken)
    per_leaf, spot = order_of(later)
    quarter = jnp.where(ramp((leaves, 128), 0) < ramp((leaves, 128), 1) * (leaves // QUARTERS), 1.0, 0.0)
    tail = dot(per_leaf, quarter.astype(BF16))[:1]
    count = tail[:, QUARTERS : QUARTERS + 1]
    row = jnp.where(source < 0, source + leaves, jnp.where(source < leaves, source + 2 * leaves, source))
    empty = 2 * leaves * leaves
    pairs = compacted(spot, row * leaves + leaf, slots * leaves, count, empty)
    spare = jnp.full((1, 128), 1.0 * empty, F32)
    listed = jnp.concatenate([pairs, spare, middle, middle_count, tail], axis=1)
    return chosen, middle.astype(jnp.int32), listed.astype(jnp.int32)


def exchange_kernel(
    grid_shape,
    far_leaf_hbm,
    far_cluster_hbm,
    near_list_hbm,
    near_count_hbm,
    top_transfer_hbm,
    top_coupling_hbm,
    points_hbm,
    charges_hbm,
    basis_hbm,
    leaf_maps_hbm,
    parent_maps_hbm,
    parent_couplings_hbm,
    leaf_couplings_hbm,
    pairs,
    side_points,
    side_charges,
    partial_hbm,
    columns_hbm,
    extra_hbm,
    far_leaf,
    far_cluster,
    near_list,
    near_count,
    top_transfer,
    top_coupling,
    partial,
    source_points,
    columns,
    own_points,
    wide_moments,
    wide_parents,
    own_charges,
    basis,
    leaf_maps,
    parent_maps,
    parent_couplings,
    leaf_couplings,
    moment_table,
    parent_table,
    far,
    local,
    sent,
    in_row,
    in_column,
    tree,
    chosen,
    early_source,
    send_sem,
    recv_sem,
    row_send,
    row_recv,
    column_send,
    column_recv,
    own_sem,
    side_sem,
    near_points,
    extra,
):
    across, along = grid_shape
    total = across * along
    me = lax.axis_index("gx") * along + lax.axis_index("gy")
    leaves, rhs, size = partial.shape
    rank = basis.shape[1]
    parents = leaf_maps.shape[0]
    links = leaves // parents

    def place(index):
        return (index // along, index % along)

    barrier = pltpu.get_barrier_semaphore()

    row, column = lax.axis_index("gx"), lax.axis_index("gy")

    def beside(step):
        return (row, (column + step) % along)

    def across_from(step):
        return ((row + step) % across, column)

    for step in range(1, along):
        pl.semaphore_signal(barrier, inc=1, device_id=beside(step), device_id_type=MESH)
    for step in range(1, across):
        pl.semaphore_signal(barrier, inc=1, device_id=across_from(step), device_id_type=MESH)
    first_of_row = (column == 0) & (row > 0)
    last_of_row = (column == along - 1) & (row < across - 1)

    @pl.when(first_of_row)
    def _():
        pl.semaphore_signal(barrier, inc=1, device_id=(row - 1, along - 1), device_id_type=MESH)

    @pl.when(last_of_row)
    def _():
        pl.semaphore_signal(barrier, inc=1, device_id=(row + 1, 0), device_id_type=MESH)
    own = [
        pltpu.make_async_copy(source, target, own_sem.at[index])
        for index, (source, target) in enumerate(
            (
                (points_hbm, own_points),
                (charges_hbm, own_charges.at[pl.ds(0, leaves)]),
                (basis_hbm, basis),
                (leaf_maps_hbm, leaf_maps),
                (parent_maps_hbm, parent_maps),
                (parent_couplings_hbm, parent_couplings),
                (leaf_couplings_hbm, leaf_couplings),
                (near_list_hbm, near_list),
                (near_count_hbm, near_count),
                (far_leaf_hbm, far_leaf),
                (far_cluster_hbm, far_cluster),
                (top_transfer_hbm, top_transfer),
                (top_coupling_hbm, top_coupling),
            )
        )
    ]
    for copy in own:
        copy.start()

    moments_of = wide_moments.shape[1]
    half = leaves // 2

    cuts = (0, leaves // FIRST, half, leaves)

    def part_of(ref, side, part):
        low, high = cuts[part], cuts[part + 1]
        return ref.at[pl.ds(leaves - high if side == 0 else low, high - low)]

    def charge_parts(part):
        sources = [part_of(charges_hbm, side, part) for side in range(2)]
        return sources, [part_of(side_charges.at[side], side, part) for side in range(2)]

    flows = (
        charge_parts(0),
        ([points_hbm] * 2, [side_points.at[side] for side in range(2)]),
        ([wide_parents.at[2]] * 2, [wide_parents.at[side] for side in range(2)]),
        ([wide_moments.at[2]] * 2, [wide_moments.at[side] for side in range(2)]),
        charge_parts(1),
        charge_parts(2),
    )

    def rightward(index):
        return pltpu.make_async_remote_copy(
            src_ref=flows[index][0][0],
            dst_ref=flows[index][1][0],
            send_sem=send_sem.at[index, 0],
            recv_sem=recv_sem.at[index, 0],
            device_id=place(jnp.minimum(me + 1, total - 1)),
            device_id_type=MESH,
        )

    def leftward(index):
        return pltpu.make_async_remote_copy(
            src_ref=flows[index][0][1],
            dst_ref=flows[index][1][1],
            send_sem=send_sem.at[index, 1],
            recv_sem=recv_sem.at[index, 1],
            device_id=place(jnp.maximum(me - 1, 0)),
            device_id_type=MESH,
        )

    def to_row(step):
        return pltpu.make_async_remote_copy(
            src_ref=sent.at[0],
            dst_ref=in_row.at[column],
            send_sem=row_send.at[step],
            recv_sem=row_recv.at[column],
            device_id=beside(step),
            device_id_type=MESH,
        )

    def from_row(step):
        source = (column + step) % along
        return pltpu.make_async_remote_copy(
            src_ref=sent.at[0],
            dst_ref=in_row.at[source],
            send_sem=row_send.at[step],
            recv_sem=row_recv.at[source],
            device_id=beside(step),
            device_id_type=MESH,
        )

    def to_column(step):
        return pltpu.make_async_remote_copy(
            src_ref=sent.at[1],
            dst_ref=in_column.at[row],
            send_sem=column_send.at[step],
            recv_sem=column_recv.at[row],
            device_id=across_from(step),
            device_id_type=MESH,
        )

    def from_column(step):
        source = (row + step) % across
        return pltpu.make_async_remote_copy(
            src_ref=sent.at[1],
            dst_ref=in_column.at[source],
            send_sem=column_send.at[step],
            recv_sem=column_recv.at[source],
            device_id=across_from(step),
            device_id_type=MESH,
        )

    def tree_level(value, index, nodes, couple):
        side = index % 2
        tree[:nodes] = value.reshape(nodes, rhs, rank)
        couple.append((side, dot(tree[index + 1 - 2 * side], top_coupling[side])))
        pair = value.reshape(nodes // 2, 2 * rhs, rank)
        lower = pair[:, :rhs].reshape(nodes // 2 * rhs, rank)
        upper = pair[:, rhs:].reshape(nodes // 2 * rhs, rank)
        return (dot(lower, top_transfer[0]) + dot(upper, top_transfer[1])).astype(BF16)

    def send(indices):
        @pl.when(me < total - 1)
        def _():
            for index in indices:
                rightward(index).start()

        @pl.when(me > 0)
        def _():
            for index in indices:
                leftward(index).start()

    def settle(indices):
        @pl.when(me < total - 1)
        def _():
            for index in indices:
                rightward(index).wait_send()
                leftward(index).wait_recv()

        @pl.when(me > 0)
        def _():
            for index in indices:
                leftward(index).wait_send()
                rightward(index).wait_recv()

    corners = jnp.where(first_of_row | last_of_row, 1, 0)
    pl.semaphore_wait(barrier, along + across - 2 + corners)
    send((1, 0))

    maps = [[spread_map(parity, rank, links, side) for side in range(2)] for parity in range(2)]
    plain = [spread_map(parity, rank, links, 0)[:rank] for parity in range(2)]
    lanes = rank // 2 * links
    mask = link_mask(links * rhs, links, lanes, rhs)
    lane = lax.broadcasted_iota(jnp.int32, (2 * rhs, lanes), 1) % links
    masks = [jnp.where(lane == link, 1.0, 0.0).astype(BF16) for link in range(links)]

    own[1].wait()
    own[2].wait()
    group = 4

    def one_moment(step, carry):
        for inner in range(group):
            leaf = step * group + inner
            pair = [dot(own_charges[at], basis[at], 1, 1) for at in (leaf, leaf + half)]
            value = jnp.concatenate(pair, axis=1).astype(BF16)
            wide_moments[2, pl.ds(pl.multiple_of(leaf * rhs, rhs), rhs), :] = value
        return carry

    lax.fori_loop(0, half // group, one_moment, 0)
    own[3].wait()
    raised = []
    for parent in range(parents):
        first = parent * links * rhs % moments_of
        stack = wide_moments[2, first : first + links * rhs, :]
        wide = [dot(stack, maps[parity][parent * links // half]) for parity in range(2)]
        product = dot(gathered_up(wide, mask, links, rhs), leaf_maps[parent])
        raised.append(fold(product, rhs, rank))
    for parent in range(parents // 2):
        value = jnp.concatenate([raised[parent], raised[parent + parents // 2]], axis=1).astype(BF16)
        wide_parents[2, parent * rhs : (parent + 1) * rhs, :] = value
    own[4].wait()
    stack = wide_parents[2]
    wide = [jnp.concatenate([dot(stack, side) for side in sides], axis=0) for sides in maps]
    product = dot(gathered_up(wide, mask, parents, rhs), parent_maps[...])
    moment = fold(product, rhs, rank).astype(BF16)
    sent[0] = moment
    for step in range(1, along):
        to_row(step).start()
    send((2, 3))

    @pl.when(me == 0)
    def _():
        wide_moments[0] = jnp.zeros(wide_moments.shape[1:], BF16)
        wide_parents[0] = jnp.zeros(wide_parents.shape[1:], BF16)

    @pl.when(me == total - 1)
    def _():
        wide_moments[1] = jnp.zeros(wide_moments.shape[1:], BF16)
        wide_parents[1] = jnp.zeros(wide_parents.shape[1:], BF16)

    own[7].wait()
    own[8].wait()
    picked, middle, listed = plan(near_list[...], near_count[...], me * leaves, leaves)
    pairs[...] = listed
    for index, value in enumerate(picked):
        chosen[index : index + 1, :leaves] = value
    chosen[EARLY : EARLY + 1, :] = middle
    choose = pltpu.make_async_copy(chosen, early_source, own_sem.at[len(own)])
    choose.start()

    own_charges[leaves] = jnp.zeros((rhs, size), BF16)
    own[0].wait()
    put_points(source_points, own_points, 0)
    source_points[leaves] = jnp.zeros(source_points.shape[1:], F32)

    def one_column(step, carry):
        for inner in range(group):
            leaf = step * group + inner
            put_columns(columns, source_points, leaf, leaf)
        return carry

    lax.fori_loop(0, leaves // group, one_column, 0)
    keep = pltpu.make_async_copy(columns, columns_hbm, own_sem.at[len(own) + 1])
    keep.start()
    choose.wait()
    batch = 4

    def own_near(step, carry):
        results = []
        for inner in range(batch):
            leaf = step * batch + inner
            found = [early_source[index, leaf] for index in range(EARLY)]
            charges = [own_charges[source] for source in found]
            results.append(near_value(columns, leaf, source_points, found, charges))
        for inner in range(batch):
            partial[step * batch + inner] = results[inner]
        return carry

    def collect(table, index, row, first):
        gathered = None
        for link in range(links):
            source = index(row, link) - first
            span = table.shape[0] // 3
            at = jnp.where(source < 0, source + span, jnp.where(source < span, source + 2 * span, source))
            at = jnp.clip(at, 0, table.shape[0] - 1)
            part = table[at] * masks[link]
            gathered = part if gathered is None else gathered + part
        return gathered

    def far_leaves():
        settle((2, 3))
        for block in range(3):
            for parity in range(2):
                for side in range(2):
                    value = dot(wide_moments[block], maps[parity][side]).astype(BF16)
                    first = block * leaves + side * half
                    rows = slice(parity * rhs, (parity + 1) * rhs)
                    moment_table[first : first + half, rows, :] = value.reshape(half, rhs, value.shape[1])
                    value = dot(wide_parents[block], maps[parity][side]).astype(BF16)
                    first = block * parents + side * parents // 2
                    value = value.reshape(parents // 2, rhs, value.shape[1])
                    parent_table[first : first + parents // 2, rows, :] = value

        own[6].wait()

        def some_leaves(step, carry):
            for inner in range(8):
                leaf = step * 8 + inner
                product = dot(collect(moment_table, lambda row, link: far_leaf[link, row], leaf, me * leaves), leaf_couplings[leaf])
                far[pl.ds(pl.multiple_of(leaf * rhs, rhs), rhs), :] = fold(product, rhs, rank)
            return carry

        lax.fori_loop(0, leaves // 8, some_leaves, 0)

    for index in range(9, 13):
        own[index].wait()
    lax.fori_loop(0, SPLIT, own_near, 0)
    for step in range(1, along):
        from_row(step).wait_send()
        from_row(step).wait_recv()
    in_row[column] = moment
    couplings = []
    value = in_row[...].reshape(along * rhs, rank)
    nodes = along
    while nodes > 1:
        value = tree_level(value, column // (along // nodes), nodes, couplings)
        nodes = nodes // 2
    sent[1] = value
    for step in range(1, across):
        to_column(step).start()
    send((4,))
    lax.fori_loop(SPLIT, leaves // batch, own_near, 0)
    for step in range(1, across):
        from_column(step).wait_send()
        from_column(step).wait_recv()
    in_column[row] = value
    value = in_column[...].reshape(across * rhs, rank)
    nodes = across
    while nodes > 1:
        value = tree_level(value, row // (across // nodes), nodes, couplings)
        nodes = nodes // 2
    send((5,))
    far_leaves()
    _, field = couplings[-1]
    for side, coupling in reversed(couplings[:-1]):
        field = coupling + ROOT_TWO * dot(field.astype(BF16), top_transfer[side], 1, 1)
    device_local = field.astype(BF16).astype(F32)

    own[5].wait()
    down = spread_down(device_local, parent_maps[...], plain, mask, links, rhs)
    parent_local = []
    for parent in range(parents):
        product = dot(collect(parent_table, lambda row, link: far_cluster[row, link], parent, me * parents), parent_couplings[parent])
        value = fold(product, rhs, rank) + down[parent * rhs : (parent + 1) * rhs]
        parent_local.append(value.astype(BF16).astype(F32))
    for parent in range(parents):
        down = spread_down(parent_local[parent], leaf_maps[parent], plain, mask, links, rhs)
        rows = slice(parent * links * rhs, (parent + 1) * links * rhs)
        local[rows, :] = (far[rows, :] + down).astype(BF16)

    def finish(step, carry):
        for inner in range(8):
            leaf = step * 8 + inner
            value = local[pl.ds(pl.multiple_of(leaf * rhs, rhs), rhs), :]
            partial[leaf] = partial[leaf] + dot(value, basis[leaf])
        return carry

    settle((1, 0, 4))

    def near_side(side):
        rows = pl.ds(leaves - half if side == 0 else 0, half)
        held = pl.ds(leaves + 1 + side * half, half)
        return (
            pltpu.make_async_copy(side_charges.at[side, rows], own_charges.at[held], side_sem.at[side, 0]),
            pltpu.make_async_copy(side_points.at[side], near_points.at[side], side_sem.at[side, 1]),
        )

    @pl.when(me > 0)
    def _():
        for copy in near_side(0):
            copy.start()

    @pl.when(me < total - 1)
    def _():
        for copy in near_side(1):
            copy.start()

    lax.fori_loop(0, leaves // 8, finish, 0)
    result = pltpu.make_async_copy(partial, partial_hbm, own_sem.at[len(own)])
    result.start()

    @pl.when(me > 0)
    def _():
        for copy in near_side(0):
            copy.wait()
        put_points(source_points, near_points.at[0, :, leaves - half :], leaves + 1)

    @pl.when(me < total - 1)
    def _():
        for copy in near_side(1):
            copy.wait()
        put_points(source_points, near_points.at[1, :, :half], leaves + 1 + half)

    def some_middle(step, carry):
        results = []
        for inner in range(GROUP):
            code = jnp.clip(early_source[EARLY, step * GROUP + inner], 0, (2 * leaves + 1) * leaves - 1)
            source = code // leaves
            results.append(near_value(columns, code % leaves, source_points, [source], [own_charges[source]]))
        for inner in range(GROUP):
            extra[step * GROUP + inner] = results[inner]
        return carry

    halfway = MIDDLE // GROUP // 2
    moved = []
    for index, (low, high) in enumerate(((0, halfway), (halfway, MIDDLE // GROUP))):
        lax.fori_loop(low, high, some_middle, 0)
        rows = pl.ds(low * GROUP, (high - low) * GROUP)
        move = pltpu.make_async_copy(extra.at[rows], extra_hbm.at[rows], own_sem.at[len(own) + 2 + index])
        move.start()
        moved.append(move)
    settle((5,))
    for move in moved:
        move.wait()
    result.wait()
    keep.wait()


def near_kernel(
    pairs,
    points_hbm,
    charges_hbm,
    side_points_hbm,
    side_charges_hbm,
    partial_hbm,
    columns_hbm,
    extra_hbm,
    potential,
    points,
    charges,
    source_points,
    columns,
    extra,
    sem,
):
    leaves, rhs, size = potential.shape
    tail = pairs.shape[1] - 128
    count = pairs[0, tail + QUARTERS]
    span = leaves // QUARTERS
    steps = [(columns_hbm.at[pl.ds(at, span)], columns.at[pl.ds(at, span)]) for at in range(0, leaves, span)]
    moves = [
        (points_hbm, points.at[2]),
        (side_points_hbm, points.at[pl.ds(0, 2)]),
        (partial_hbm, potential),
        (extra_hbm, extra),
        steps[0],
        (side_charges_hbm.at[0], charges.at[pl.ds(0, leaves)]),
        (side_charges_hbm.at[1], charges.at[pl.ds(leaves, leaves)]),
        (charges_hbm, charges.at[pl.ds(2 * leaves, leaves)]),
    ] + steps[1:]
    copies = [
        pltpu.make_async_copy(source, target, sem.at[index]) for index, (source, target) in enumerate(moves)
    ]
    for copy in copies:
        copy.start()
    copies[0].wait()
    copies[1].wait()
    for block in range(3):
        put_points(source_points, points.at[block], block * leaves)
    copies[2].wait()
    copies[3].wait()

    def one_extra(index, carry):
        target = pairs[0, tail - 256 + index] % leaves
        potential[target] = potential[target] + extra[index]
        return carry

    lax.fori_loop(0, pairs[0, tail - 128], one_extra, 0)
    for copy in copies[4:8]:
        copy.wait()

    def some_pairs(step, carry):
        results = []
        for inner in range(GROUP):
            at = step * GROUP + inner
            code = pairs[0, at]
            source = code // leaves
            target = code % leaves
            value = near_value(columns, target, source_points, [source], [charges[source]])
            results.append((target, jnp.where(at < count, value, 0.0)))
        for target, value in results:
            potential[target] = potential[target] + value
        return carry

    done = 0
    for quarter in range(QUARTERS):
        if quarter > 0:
            copies[7 + quarter].wait()
        bound = pairs[0, tail + 1 + quarter] // GROUP if quarter < QUARTERS - 1 else (count + GROUP - 1) // GROUP
        lax.fori_loop(done, bound, some_pairs, 0)
        done = bound


def stored(matrix, links):
    length = matrix.shape[-1]
    tiles = length // 128
    value = matrix.reshape(-1, links, tiles, 128).transpose(0, 2, 1, 3)
    return value.reshape(-1, tiles * links, 128)


def on_device(
    grid_shape,
    points,
    charges,
    near_list,
    near_count,
    far_leaf,
    far_cluster,
    basis,
    leaf_transfer,
    cluster_transfer,
    leaf_coupling,
    cluster_coupling,
    top_transfer,
    top_coupling,
):
    leaves, rhs, size = charges.shape
    rank = basis.shape[1]
    parents = cluster_transfer.shape[0]
    links = far_leaf.shape[1]
    slots = near_list.shape[1]
    across, along = grid_shape
    turned = points.transpose(1, 0, 2)
    leaf_maps = stored(leaf_transfer, links)
    parent_maps = stored(cluster_transfer, links)[0]
    leaf_couplings = stored(leaf_coupling, links)
    parent_couplings = stored(cluster_coupling, links)
    hbm = pl.BlockSpec(memory_space=pl.ANY)
    shape = jax.ShapeDtypeStruct
    spread = rank // 2 * links
    length = slots * leaves + 4 * 128
    count_row = near_count.reshape(1, leaves)
    pairs, side_points, side_charges, partial, columns, extra = pl.pallas_call(
        functools.partial(exchange_kernel, grid_shape),
        out_shape=(
            shape((1, length), jnp.int32),
            shape((2,) + turned.shape, BF16),
            shape((2,) + charges.shape, BF16),
            shape((leaves, rhs, size), F32),
            shape((leaves, 3, size, 128), BF16),
            shape((MIDDLE, rhs, size), F32),
        ),
        in_specs=[hbm] * 13,
        out_specs=(pl.BlockSpec(memory_space=pltpu.VMEM), hbm, hbm, hbm, hbm, hbm),
        scratch_shapes=[
            pltpu.SMEM((links, leaves), jnp.int32),
            pltpu.SMEM((parents, links), jnp.int32),
            pltpu.VMEM((slots, leaves), jnp.int32),
            pltpu.VMEM((1, leaves), jnp.int32),
            pltpu.VMEM(top_transfer.shape, BF16),
            pltpu.VMEM(top_coupling.shape, BF16),
            pltpu.VMEM((leaves, rhs, size), F32),
            pltpu.VMEM((2 * leaves + 1, 8, size), F32),
            pltpu.VMEM((leaves, 3, size, 128), BF16),
            pltpu.VMEM(turned.shape, BF16),
            pltpu.VMEM((3, leaves // 2 * rhs, 2 * rank), BF16),
            pltpu.VMEM((3, parents // 2 * rhs, 2 * rank), BF16),
            pltpu.VMEM((2 * leaves + 1, rhs, size), BF16),
            pltpu.VMEM(basis.shape, BF16),
            pltpu.VMEM(leaf_maps.shape, BF16),
            pltpu.VMEM(parent_maps.shape, BF16),
            pltpu.VMEM(parent_couplings.shape, BF16),
            pltpu.VMEM(leaf_couplings.shape, BF16),
            pltpu.VMEM((3 * leaves, 2 * rhs, spread), BF16),
            pltpu.VMEM((3 * parents, 2 * rhs, spread), BF16),
            pltpu.VMEM((leaves * rhs, rank), F32),
            pltpu.VMEM((leaves * rhs, rank), BF16),
            pltpu.VMEM((2, rhs, rank), BF16),
            pltpu.VMEM((along, rhs, rank), BF16),
            pltpu.VMEM((across, rhs, rank), BF16),
            pltpu.VMEM((max(along, across), rhs, rank), BF16),
            pltpu.VMEM((8, 128), jnp.int32),
            pltpu.SMEM((8, 128), jnp.int32),
            pltpu.SemaphoreType.DMA((6, 2)),
            pltpu.SemaphoreType.DMA((6, 2)),
            pltpu.SemaphoreType.DMA((along,)),
            pltpu.SemaphoreType.DMA((along,)),
            pltpu.SemaphoreType.DMA((across,)),
            pltpu.SemaphoreType.DMA((across,)),
            pltpu.SemaphoreType.DMA((17,)),
            pltpu.SemaphoreType.DMA((2, 2)),
            pltpu.VMEM((2,) + turned.shape, BF16),
            pltpu.VMEM((MIDDLE, rhs, size), F32),
        ],
        compiler_params=pltpu.CompilerParams(
            collective_id=0, has_side_effects=True, vmem_limit_bytes=EXCHANGE_MIB << 20
        ),
        name="exchange",
    )(
        far_leaf.T,
        far_cluster,
        near_list.T,
        count_row,
        top_transfer,
        top_coupling,
        turned,
        charges,
        basis,
        leaf_maps,
        parent_maps,
        parent_couplings,
        leaf_couplings,
    )
    return pl.pallas_call(
        near_kernel,
        out_shape=shape((leaves, rhs, size), F32),
        in_specs=[pl.BlockSpec(memory_space=pltpu.SMEM)] + [hbm] * 7,
        out_specs=pl.BlockSpec(memory_space=pltpu.VMEM),
        scratch_shapes=[
            pltpu.VMEM((3,) + turned.shape, BF16),
            pltpu.VMEM((3 * leaves, rhs, size), BF16),
            pltpu.VMEM((3 * leaves, 8, size), F32),
            pltpu.VMEM((leaves, 3, size, 128), BF16),
            pltpu.VMEM((MIDDLE, rhs, size), F32),
            pltpu.SemaphoreType.DMA((7 + QUARTERS,)),
        ],
        compiler_params=pltpu.CompilerParams(vmem_limit_bytes=NEAR_MIB << 20),
        name="near",
    )(pairs, turned, charges, side_points, side_charges, partial, columns, extra)


def solution(mesh):
    grid_shape = (mesh.shape["gx"], mesh.shape["gy"])
    both = ("gx", "gy")
    in_specs = (
        P(both, None, None),
        P(both, None, None),
        P(both, None),
        P(both),
        P(both, None),
        P(both, None),
        P(both, None, None),
        P(both, None),
        P(both, None),
        P(both, None, None),
        P(both, None, None),
        P(),
        P(),
    )
    return jax.shard_map(
        functools.partial(on_device, grid_shape),
        mesh=mesh,
        in_specs=in_specs,
        out_specs=P(both, None, None),
        check_vma=False,
    )
```
